32 devices in a mesh: slab: 4 (over y, x), member: 8 (over z, core).
Axes of the slice: x: 2, y: 2, z: 4, core: 2. Of those that a mesh axis runs over, the one named last changes fastest.
Arguments:
- prior_sample_group: float32 [64, 64, 3, 512], P('member', 'slab'), may hold values from -6 to 6
- obs_values: float32 [4, 256], replicated, may hold values from -6 to 6
- obs_variance: float32 [4, 256], replicated, may hold values from 0.25 to 4
- obs_perturb: float32 [4, 256, 64], replicated, may hold values from -6 to 6
- obs_offset: int32 [4, 256], replicated, may hold values from 0 to 8191
- owner_order: int32 [4], replicated, may hold values from 0 to 3, each once
- taper_cutoff: int32 [4, 256], replicated, may hold values from 32 to 64
Outputs:
- analysis: float32 [64, 98304], P(None, ('slab', 'member'))
The draws below stay inside these ranges and needn't reach their ends.
Inputs may be any that keep to these rules, and one draw needn't show every extreme that they name: A permutation of the slab indices; batch b belongs to slab owner_order[b mod the number of slabs]. `obs_offset`: row-major offset within the owner slab's block of 16 x 512 cells.
All inputs are finite; a program needn't handle non-finite values.
Results may differ from the reference program's by a relative error of at most 0.0003.
Values sent between devices are 32-bit elements; how exact they have to be, the bound alone decides.
No kernel may reach another device: no remote copies, remote signals or barrier semaphores. Data moves between devices by JAX's collectives and lax.ppermute only.
A program may use at most 64 MiB of HBM per device.

```python
import math
import jax
import jax.numpy as jnp
from jax import lax

CX = 16
NY = 512
NOBS = 256
NBATCH = 4
ENSEMBLE_SIZE = 64
NX = 64
N_SLAB = 4


def plant(values, key, low, high):
    index_at = [jax.random.randint(jax.random.fold_in(key, axis), (), 0, length) for axis, length in enumerate(values.shape)]
    longest = values.shape.index(max(values.shape))
    neighbour = index_at[:longest] + [(index_at[longest] + 1) % values.shape[longest]] + index_at[longest + 1:]
    return values.at[tuple(index_at)].set(low).at[tuple(neighbour)].set(high)


def block_scale(key, shape, pieces, low, high):
    loudness = 1.0
    for dim, parts in pieces:
        heights = jax.random.uniform(jax.random.fold_in(jax.random.fold_in(key, 6), dim), (parts,), jnp.float32, low / len(pieces), high / len(pieces))
        loudness = loudness * jnp.repeat(jnp.exp(heights), shape[dim] // parts).reshape((-1,) + (1,) * (len(shape) - 1 - dim))
    return loudness


def scatter_about(key, dims, deviation, most, pieces=(), held_as=jnp.bfloat16):
    level = block_scale(key, dims, pieces, -0.22, 0.18) if pieces else 1.0
    entries = jax.random.normal(key, dims, jnp.float32) * deviation * level
    return jnp.minimum(jnp.maximum(entries, -most), most).astype(held_as)


def setup_inputs(seed: int = 0) -> dict:
    seeds = jax.random.split(jax.random.key(seed), 8)
    return {
        "prior_sample_group": scatter_about(seeds[0], (ENSEMBLE_SIZE, NX, 3, NY), 1.0, 6.0, ((0, 8), (1, 4)), jnp.float32),
        "obs_values": scatter_about(seeds[1], (NBATCH, NOBS), 1.0, 6.0, (), jnp.float32),
        "obs_variance": jnp.clip(jnp.exp(jax.random.uniform(seeds[2], (NBATCH, NOBS), jnp.float32, math.log(0.25), math.log(4.0))), 0.25, 4.0),
        "obs_perturb": scatter_about(seeds[3], (NBATCH, NOBS, ENSEMBLE_SIZE), 1.0, 6.0, (), jnp.float32),
        "obs_offset": plant(jax.random.randint(seeds[4], (NBATCH, NOBS), 0, CX * NY), jax.random.fold_in(seeds[4], 1), 0, (CX * NY) - 1).astype(jnp.int32),
        "owner_order": jax.random.permutation(seeds[5], N_SLAB).astype(jnp.int32),
        "taper_cutoff": plant(jax.random.randint(seeds[6], (NBATCH, NOBS), NX // 2, NX + 1), jax.random.fold_in(seeds[6], 1), NX // 2, NX).astype(jnp.int32),
    }


courant = 0.3
rotation = 0.1

def centred_y(sample):
    return (jnp.roll(sample, -1, axis=2) - jnp.roll(sample, 1, axis=2)) * 0.5

def fluid_layer_timestep(extended):
    height = extended[:, :, 0]
    velocity_x = extended[:, :, 1]
    velocity_y = extended[:, :, 2]
    spread = (velocity_x[:, 2:] - velocity_x[:, :-2]) * 0.5 + centred_y(velocity_y)[:, 1:-1]
    new_height = height[:, 1:-1] - courant * spread
    slope_x = (new_height[:, 2:] - new_height[:, :-2]) * 0.5
    slope_y = centred_y(new_height)[:, 1:-1]
    new_x = velocity_x[:, 2:-2] - courant * slope_x + rotation * velocity_y[:, 2:-2]
    new_y = velocity_y[:, 2:-2] - courant * slope_y - rotation * velocity_x[:, 2:-2]
    return jnp.stack([new_height[:, 1:-1], new_x, new_y], axis=2)

def observe_layout(offsets, owner_slab, cells_x, cells_y):
    cell_index = owner_slab * (cells_x * cells_y) + offsets
    obs_row = cell_index // cells_y
    column = cell_index % cells_y
    return (obs_row, column, obs_row * (3 * cells_y) + column)

def taper_weights(var_index, obs_row, obs_column, cutoff, total_x, cells_y):
    var_row = var_index // (3 * cells_y)
    var_column = var_index % cells_y
    gap_x = jnp.abs(var_row[:, None] - obs_row[None, :])
    gap_x = jnp.minimum(gap_x, total_x - gap_x)
    gap_y = jnp.abs(var_column[:, None] - obs_column[None, :])
    gap_y = jnp.minimum(gap_y, cells_y - gap_y)
    distance = jnp.sqrt((gap_x * gap_x + gap_y * gap_y).astype(jnp.float32))
    return jnp.square(jnp.maximum(0.0, 1.0 - distance / cutoff.astype(jnp.float32)[None, :]))

def solve_batch(observed, values_in, variance, perturb):
    members = observed.shape[1]
    spread = observed - lax.optimization_barrier(jnp.mean(observed, axis=1, keepdims=True))
    system = jnp.dot(spread, spread.T, precision=lax.Precision.HIGHEST) / (members - 1) + jnp.diag(variance)
    target = values_in[:, None] + jnp.sqrt(variance)[:, None] * perturb - observed
    factor = jnp.linalg.cholesky(system)
    forward = lax.linalg.triangular_solve(factor, target, left_side=True, lower=True)
    weights = lax.linalg.triangular_solve(factor, forward, left_side=True, lower=True, transpose_a=True)
    return (spread, weights)

def apply_batch(system_quantities, spread, weights, taper_rho):
    members = system_quantities.shape[0]
    anomaly = system_quantities - lax.optimization_barrier(jnp.mean(system_quantities, axis=0, keepdims=True))
    covariance = lax.dot_general(anomaly, spread, (((0,), (1,)), ((), ())), precision=lax.Precision.HIGHEST) / (members - 1)
    local_gain = covariance * taper_rho
    return system_quantities + lax.dot_general(weights, local_gain, (((0,), (1,)), ((), ())), precision=lax.Precision.HIGHEST)

def reference(prior_sample_group, obs_values, obs_variance, obs_perturb, obs_offset, owner_order, taper_cutoff):
    predict_ahead = prior_sample_group
    for repeat in range(2):
        bordered_grid = jnp.concatenate([predict_ahead[:, -2:], predict_ahead, predict_ahead[:, :2]], axis=1)
        predict_ahead = fluid_layer_timestep(bordered_grid)
    strip_quantities = 3 * CX * NY
    system_quantities = predict_ahead.reshape(ENSEMBLE_SIZE, N_SLAB * strip_quantities)
    for batch_no in range(NBATCH):
        owner_slab = owner_order[batch_no % N_SLAB]
        obs_row, obs_column, obs_flat = observe_layout(obs_offset[batch_no], owner_slab, CX, NY)
        observed = system_quantities[:, obs_flat].T
        spread, weights = solve_batch(observed, obs_values[batch_no], obs_variance[batch_no], obs_perturb[batch_no])
        cutoff = taper_cutoff[batch_no]

        def update_slab(slab_no, current=system_quantities, spread=spread, weights=weights, obs_row=obs_row, obs_column=obs_column, cutoff=cutoff):
            first_var = (slab_no * strip_quantities).astype(jnp.int32)
            block = lax.dynamic_slice_in_dim(current, first_var, strip_quantities, 1)
            var_index = first_var + lax.iota(jnp.int32, strip_quantities)
            taper_rho = taper_weights(var_index, obs_row, obs_column, cutoff, CX * N_SLAB, NY)
            return apply_batch(block, spread, weights, taper_rho)
        updated = lax.map(update_slab, jnp.arange(N_SLAB, dtype=jnp.int32))
        system_quantities = jnp.transpose(updated, (1, 0, 2)).reshape(ENSEMBLE_SIZE, N_SLAB * strip_quantities)
    return system_quantities
```

```python
import functools
import math

import jax
import jax.numpy as jnp
from jax import lax
from jax.experimental import pallas as pl
from jax.experimental.pallas import tpu as pltpu
from jax.sharding import PartitionSpec as P

COURANT = 0.3
ROTATION = 0.1
HALF = COURANT * 0.5
F32 = jnp.float32
BF16 = jnp.bfloat16
VMEM_SPEC = pl.BlockSpec(memory_space=pltpu.VMEM)
SMEM_SPEC = pl.BlockSpec(memory_space=pltpu.SMEM)


def d_y(field):
    width = field.shape[-1]
    axis = field.ndim - 1
    return (pltpu.roll(field, width - 1, axis) - pltpu.roll(field, 1, axis)) * 0.5


def split2(x):
    high = x.astype(BF16)
    return high, (x - high.astype(F32)).astype(BF16)


def mm(a, b):
    return lax.dot_general(a, b, (((1,), (0,)), ((), ())), preferred_element_type=F32)


def mm_f32(a, b, dims=((1,), (0,))):
    return lax.dot_general(
        a, b, (dims, ((), ())), precision=lax.Precision.HIGHEST, preferred_element_type=F32
    )


def keep_lanes(ref, start, value):
    rows, width = value.shape
    for c in range(width // 128):
        ref[c, start : start + rows, :] = value[:, c * 128 : (c + 1) * 128]


def every_nth(ref, start, count, stride):
    return jnp.concatenate(
        [ref[c, pl.ds(start, count, stride=stride), :] for c in range(ref.shape[0])], axis=1)


def row_up(field, edge, index):
    rows = field.shape[0]
    return jnp.where(index == rows - 1, edge, pltpu.roll(field, rows - 1, 0))


def row_down(field, edge, index):
    return jnp.where(index == 0, edge, pltpu.roll(field, 1, 0))


def wave_twice(h, u, v, low, high, velocities):
    rows = h.shape[0]
    index = lax.broadcasted_iota(jnp.int32, h.shape, 0)
    u_low, q_low, r_low, s_low = low
    u_high, q_high, r_high, s_high = high
    h1 = h - HALF * (row_up(u, u_high, index) - row_down(u, u_low, index)) - COURANT * d_y(v)
    h1_low = q_low - HALF * u[0:1]
    h1_high = q_high + HALF * u[rows - 1 : rows]
    u1 = u - HALF * (row_up(h1, h1_high, index) - row_down(h1, h1_low, index)) + ROTATION * v
    v1 = v - COURANT * d_y(h1) - ROTATION * u
    u1_low = r_low - HALF * h1[0:1]
    u1_high = r_high + HALF * h1[rows - 1 : rows]
    h2 = h1 - HALF * (row_up(u1, u1_high, index) - row_down(u1, u1_low, index)) - COURANT * d_y(v1)
    if not velocities:
        return h2
    keep = 1.0 - HALF * HALF
    square = COURANT * COURANT
    h2_low = keep * h1_low + square * d_y(d_y(h1_low)) + s_low - HALF * u1[0:1]
    h2_high = keep * h1_high + square * d_y(d_y(h1_high)) + s_high + HALF * u1[rows - 1 : rows]
    u2 = u1 - HALF * (row_up(h2, h2_high, index) - row_down(h2, h2_low, index)) + ROTATION * v1
    v2 = v1 - COURANT * d_y(h2) - ROTATION * u1
    return h2, u2, v2


def edge_rows(h, u, v, sign):
    a = sign * HALF
    dv0 = COURANT * d_y(v[0])
    q = h[0] + a * u[1] - dv0
    h1_1 = h[1] - a * (u[0] - u[2]) - COURANT * d_y(v[1])
    r = u[0] + a * h1_1 + ROTATION * v[0]
    h1_2 = h[2] - a * (u[1] - u[3]) - COURANT * d_y(v[2])
    p = u[1] + a * h1_2 + ROTATION * v[1]
    s = a * p - dv0 + COURANT * ROTATION * d_y(u[0])
    h1 = a * u[0]
    first = (1.0 - 2.0 * HALF * HALF) * h1 + a * r + COURANT * COURANT * d_y(d_y(h1))
    return (u[0], q, r, s), (first, HALF * HALF * q, HALF * HALF * h1)


def prior_kernel(members, cells_x, slabs, batches, me_ref, owner_ref, x_ref, offset_ref,
                 obs_ref, low_ref, high_ref, rows_ref, lanes_ref):
    cells_y = x_ref.shape[1]
    nobs = offset_ref.shape[1]
    zero = (jnp.zeros((1, cells_y), F32),) * 4
    base = members * cells_x
    for m in range(members):
        start = m * 3 * cells_x
        h, u, v = (x_ref[pl.ds(start + f * cells_x, cells_x), :] for f in range(3))
        rows_ref[pl.ds(m * cells_x, cells_x), :] = wave_twice(h, u, v, zero, zero, False)

    keep_lanes(lanes_ref, 0, x_ref[...])

    def across(field, row):
        return every_nth(lanes_ref, field * cells_x + row, members, 3 * cells_x)

    last = cells_x - 1
    sent, added = edge_rows(
        [across(0, last - i) for i in range(3)], [across(1, last - i) for i in range(4)],
        [across(2, last - i) for i in range(3)], 1.0)
    for i in range(4):
        low_ref[pl.ds(i * members, members), :] = sent[i]
    for i in range(3):
        rows_ref[pl.ds(base + i * members, members), :] = added[i]
    sent, added = edge_rows(
        [across(0, i) for i in range(3)], [across(1, i) for i in range(4)],
        [across(2, i) for i in range(3)], -1.0)
    for i in range(4):
        high_ref[pl.ds(i * members, members), :] = sent[i]
    for i in range(3):
        rows_ref[pl.ds(base + (3 + i) * members, members), :] = added[i]

    values = rows_ref[...]
    part0 = values.astype(BF16)
    rest = values - part0.astype(F32)
    part1 = rest.astype(BF16)
    part2 = (rest - part1.astype(F32)).astype(BF16)
    me = me_ref[0]
    total = cells_x * slabs
    for b in range(batches):
        offset = offset_ref[b : b + 1, :]
        column = lax.rem(offset, cells_y)
        row = lax.div(offset, cells_y)
        relative = row + lax.rem(owner_ref[b % slabs] - me + slabs, slabs) * cells_x
        pick = jnp.where(
            lax.broadcasted_iota(jnp.int32, (cells_y, nobs), 0) == column, 1.0, 0.0).astype(BF16)
        found = mm(part0, pick) + (mm(part1, pick) + mm(part2, pick))
        inside = lax.broadcasted_iota(jnp.int32, (cells_x, nobs), 0) == relative
        edges = jnp.zeros((members, nobs), F32)
        for i in range(3):
            piece = found[base + i * members : base + (i + 1) * members]
            edges += jnp.where(relative == cells_x + i, piece, 0.0)
            piece = found[base + (3 + i) * members : base + (4 + i) * members]
            edges += jnp.where(relative == total - 1 - i, piece, 0.0)
        own = [
            jnp.sum(jnp.where(inside, found[m * cells_x : (m + 1) * cells_x], 0.0),
                    axis=0, keepdims=True)
            for m in range(members)
        ]
        obs_ref[:, b * nobs : (b + 1) * nobs] = jnp.concatenate(own, axis=0) + edges


def forecast_kernel(members, cells_x, x_ref, low_ref, high_ref, out_ref, rows_ref):
    cells_y = x_ref.shape[1]
    chunk = out_ref.shape[2]
    piece = math.gcd(chunk, cells_y)
    for m in range(members):
        start = m * 3 * cells_x
        h, u, v = (x_ref[pl.ds(start + f * cells_x, cells_x), :] for f in range(3))
        low = [low_ref[pl.ds(i * members + m, 1), :] for i in range(4)]
        high = [high_ref[pl.ds(i * members + m, 1), :] for i in range(4)]
        for f, value in enumerate(wave_twice(h, u, v, low, high, True)):
            keep_lanes(rows_ref, start + f * cells_x, value)
    for r in range(cells_x):
        for f in range(3):
            line = every_nth(rows_ref, f * cells_x + r, members, 3 * cells_x)
            for c in range(0, cells_y, piece):
                flat = (r * 3 + f) * cells_y + c
                out_ref[flat // chunk, :, flat % chunk : flat % chunk + piece] = line[:, c : c + piece]


def column_of(row):
    return jnp.transpose(jnp.broadcast_to(row, (8,) + row.shape[1:]))[:, 0:1]


def taper_of(row_i, column_i, inverse_i, row_j, column_j, total_x, cells_y):
    gap_x = jnp.abs(row_j - row_i)
    gap_x = jnp.minimum(gap_x, total_x - gap_x)
    gap_y = jnp.abs(column_j - column_i)
    gap_y = jnp.minimum(gap_y, cells_y - gap_y)
    distance = jnp.sqrt(gap_x * gap_x + gap_y * gap_y)
    ramp = jnp.maximum(0.0, 1.0 - distance * inverse_i)
    return ramp * ramp


def geometry(owner_ref, offset_ref, cutoff_ref, b, slabs, cells_x, cells_y):
    offset = offset_ref[b : b + 1, :]
    row = lax.div(offset, cells_y) + owner_ref[b % slabs] * cells_x
    column = lax.rem(offset, cells_y)
    return row.astype(F32), column.astype(F32), 1.0 / cutoff_ref[b : b + 1, :].astype(F32)


def taper_kernel(slabs, cells_x, cells_y, batches, tile, groups, first_ref, owner_ref, offset_ref,
                 cutoff_ref, out_ref):
    nobs = offset_ref.shape[1]
    for b in range(batches):
        row, column, inverse = geometry(owner_ref, offset_ref, cutoff_ref, b, slabs, cells_x, cells_y)
        row, column, inverse = column_of(row), column_of(column), column_of(inverse)
        for g, at in enumerate(groups):
            start = first_ref[0] + at
            cell_row = lax.div(start, 3 * cells_y).astype(F32)
            cell_column = (lax.rem(start, cells_y) + lax.broadcasted_iota(jnp.int32, (1, tile), 1)).astype(F32)
            out_ref[b, g] = taper_of(row, column, inverse, cell_row, cell_column,
                                     float(cells_x * slabs), float(cells_y))


def chain_kernel(slabs, cells_x, cells_y, batches, parts, *refs):
    place_ref, owner_ref, offset_ref, cutoff_ref, values_ref, variance_ref, perturb_ref = refs[:7]
    part_refs = refs[7 : 7 + parts]
    y_ref, w_ref, obs_ref, aug_ref = refs[7 + parts :]
    members = obs_ref.shape[0]
    nobs = offset_ref.shape[1]
    each = part_refs[0].shape[0]
    scale = 1.0 / (members - 1)
    for k in range(parts):
        obs_ref[pl.ds(pl.multiple_of(place_ref[k] * each, each), each), :] = part_refs[k][...]
    eye = (lax.broadcasted_iota(jnp.int32, (members, members), 0)
           == lax.broadcasted_iota(jnp.int32, (members, members), 1))
    places = [geometry(owner_ref, offset_ref, cutoff_ref, b, slabs, cells_x, cells_y)
              for b in range(batches)]
    sublane = lax.broadcasted_iota(jnp.int32, (8, 2 * members), 0)
    for b in range(batches):
        observed = obs_ref[:, b * nobs : (b + 1) * nobs]
        spread = observed - jnp.mean(observed, axis=0, keepdims=True)
        variance = variance_ref[b : b + 1, :]
        inverse = 1.0 / variance
        target = values_ref[b : b + 1, :] + jnp.sqrt(variance) * perturb_ref[b] - observed
        both = mm_f32(spread * inverse, jnp.concatenate([spread, target], axis=0), ((1,), (1,)))
        gram = both[:, :members] + jnp.where(eye, float(members - 1), 0.0)
        aug_ref[:, :members] = gram
        aug_ref[:, members:] = both[:, members:]

        def eliminate(block, carry):
            at = pl.ds(pl.multiple_of(block * 8, 8), 8)
            panel = aug_ref[at, :]
            for j in range(8):
                line = panel[j : j + 1, :] * (1.0 / panel[j : j + 1, j : j + 1])
                panel = jnp.where(sublane == j, line, panel - panel[:, j : j + 1] * line)
            every = aug_ref[...]
            for j in range(8):
                every = every - every[:, j : j + 1] * panel[j : j + 1, :] if j == 0 else every - aug_ref[:, j : j + 1] * panel[j : j + 1, :]
            aug_ref[...] = every
            aug_ref[at, :] = panel
            aug_ref[...] = pltpu.roll(aug_ref[...], 2 * members - 8, 1)
            return carry

        lax.fori_loop(0, members // 8, eliminate, 0)
        solved = aug_ref[:, :members]
        weights = (target - mm_f32(solved, spread, ((0,), (0,)))) * inverse
        spread_t = jnp.transpose(spread) * scale
        high, low = split2(spread_t)
        y_ref[b] = jnp.concatenate([high, high, low], axis=1)
        high, low = split2(weights)
        w_ref[b] = jnp.concatenate([high, low], axis=0)
        if b + 1 < batches:
            later = obs_ref[:, (b + 1) * nobs :]
            anomaly = later - jnp.mean(later, axis=0, keepdims=True)
            covariance = mm_f32(spread_t, anomaly)
            row, column, inverse_cutoff = (column_of(x) for x in places[b])
            row_j = jnp.concatenate([places[c][0] for c in range(b + 1, batches)], axis=1)
            column_j = jnp.concatenate([places[c][1] for c in range(b + 1, batches)], axis=1)
            taper = taper_of(row, column, inverse_cutoff, row_j, column_j,
                             float(cells_x * slabs), float(cells_y))
            obs_ref[:, (b + 1) * nobs :] = later + mm_f32(weights, covariance * taper)


def update_kernel(batches, tile, groups, s_ref, y_ref, w_ref, taper_ref, out_ref):
    members = s_ref.shape[0]
    for g, tiles in enumerate(groups):
        state = jnp.concatenate([s_ref[:, at : at + tile] for at in tiles], axis=1)
        for b in range(batches):
            anomaly = state - jnp.mean(state, axis=0, keepdims=True)
            high, low = split2(anomaly)
            covariance = mm(y_ref[b], jnp.concatenate([high, low, high], axis=0))
            taper = taper_ref[b, g]
            gain = covariance * jnp.concatenate([taper] * len(tiles), axis=1)
            high, low = split2(gain)
            two = mm(w_ref[b], high)
            one = mm(w_ref[b, :members], low)
            state = state + (two[:members] + (two[members:] + one))
        for i, at in enumerate(tiles):
            out_ref[:, at : at + tile] = state[:, i * tile : (i + 1) * tile]


def on_device(prior, obs_values, obs_variance, obs_perturb, obs_offset, owner_order, taper_cutoff):
    slabs = lax.axis_size("slab")
    shards = lax.axis_size("member")
    each, cells_x, _, cells_y = prior.shape
    batches, nobs = obs_values.shape
    members = each * shards
    chunk = 3 * cells_x * cells_y // shards
    slab = lax.axis_index("slab")
    member = lax.axis_index("member")
    x = prior.transpose(0, 2, 1, 3).reshape(each * 3 * cells_x, cells_y)
    owner = owner_order.astype(jnp.int32)
    perturb = obs_perturb.transpose(0, 2, 1)

    def shift(count, by):
        return [(i, (i + by) % count) for i in range(count)]

    partial, low, high = pl.pallas_call(
        functools.partial(prior_kernel, each, cells_x, slabs, batches),
        out_shape=(
            jax.ShapeDtypeStruct((each, batches * nobs), F32),
            jax.ShapeDtypeStruct((4 * each, cells_y), F32),
            jax.ShapeDtypeStruct((4 * each, cells_y), F32),
        ),
        in_specs=[SMEM_SPEC, SMEM_SPEC, VMEM_SPEC, VMEM_SPEC],
        out_specs=(VMEM_SPEC,) * 3,
        scratch_shapes=[
            pltpu.VMEM((each * cells_x + 6 * each, cells_y), F32),
            pltpu.VMEM((cells_y // 128, each * 3 * cells_x, 128), F32),
        ],
        name="prior",
    )(slab.reshape(1), owner, x, obs_offset)

    observed = partial
    for by in range(1, slabs):
        observed = observed + lax.ppermute(partial, "slab", shift(slabs, by))
    low = lax.ppermute(low, "slab", shift(slabs, 1))
    high = lax.ppermute(high, "slab", shift(slabs, -1))

    pieces = [observed]
    for by in range(1, shards):
        pieces.append(lax.ppermute(observed, "member", shift(shards, by)))
    place = lax.rem(member - jnp.arange(shards, dtype=jnp.int32) + shards, shards)

    outgoing = pl.pallas_call(
        functools.partial(forecast_kernel, each, cells_x),
        out_shape=jax.ShapeDtypeStruct((shards, each, chunk), F32),
        in_specs=[VMEM_SPEC] * 3,
        out_specs=VMEM_SPEC,
        scratch_shapes=[pltpu.VMEM((cells_y // 128, each * 3 * cells_x, 128), F32)],
        name="forecast",
    )(x, low, high)
    state = lax.all_to_all(outgoing, "member", 0, 0).reshape(members, chunk)

    tile = math.gcd(chunk, 256)
    if chunk % (3 * cells_y) == 0:
        groups = [
            [r * 3 * cells_y + f * cells_y + c for f in range(3)]
            for r in range(chunk // (3 * cells_y))
            for c in range(0, cells_y, tile)
        ]
    else:
        groups = [[at] for at in range(0, chunk, tile)]
    first = (slab * shards + member) * chunk
    taper = pl.pallas_call(
        functools.partial(taper_kernel, slabs, cells_x, cells_y, batches, tile, [g[0] for g in groups]),
        out_shape=jax.ShapeDtypeStruct((batches, len(groups), nobs, tile), F32),
        in_specs=[SMEM_SPEC, SMEM_SPEC, VMEM_SPEC, VMEM_SPEC],
        out_specs=VMEM_SPEC,
        name="taper",
    )(first.reshape(1), owner, obs_offset, taper_cutoff)

    y_all, w_all = pl.pallas_call(
        functools.partial(chain_kernel, slabs, cells_x, cells_y, batches, shards),
        out_shape=(
            jax.ShapeDtypeStruct((batches, nobs, 3 * members), BF16),
            jax.ShapeDtypeStruct((batches, 2 * members, nobs), BF16),
        ),
        in_specs=[SMEM_SPEC, SMEM_SPEC] + [VMEM_SPEC] * (5 + shards),
        out_specs=(VMEM_SPEC,) * 2,
        scratch_shapes=[
            pltpu.VMEM((members, batches * nobs), F32),
            pltpu.VMEM((members, 2 * members), F32),
        ],
        name="chain",
    )(place, owner, obs_offset, taper_cutoff, obs_values, obs_variance, perturb, *pieces)

    return pl.pallas_call(
        functools.partial(update_kernel, batches, tile, groups),
        out_shape=jax.ShapeDtypeStruct((members, chunk), F32),
        in_specs=[VMEM_SPEC] * 4,
        out_specs=VMEM_SPEC,
        name="update",
    )(state, y_all, w_all, taper)


def solution(mesh):
    in_specs = (P("member", "slab", None, None), P(), P(), P(), P(), P(), P())
    out_specs = P(None, ("slab", "member"))
    return jax.shard_map(
        on_device, mesh=mesh, in_specs=in_specs, out_specs=out_specs, check_vma=False
    )
```

```python
import functools
import math

import jax
import jax.numpy as jnp
from jax import lax
from jax.experimental import pallas as pl
from jax.experimental.pallas import tpu as pltpu
from jax.sharding import PartitionSpec as P


COURANT = 0.3
ROTATION = 0.1
HALF = COURANT * 0.5
ROUNDS = 6
CONVERGED = 1e6
F32 = jnp.float32
BF16 = jnp.bfloat16
VMEM_SPEC = pl.BlockSpec(memory_space=pltpu.VMEM)
SMEM_SPEC = pl.BlockSpec(memory_space=pltpu.SMEM)


def d_y(field):
    width = field.shape[-1]
    axis = field.ndim - 1
    return (pltpu.roll(field, width - 1, axis) - pltpu.roll(field, 1, axis)) * 0.5


def split2(x):
    high = x.astype(BF16)
    return high, (x - high.astype(F32)).astype(BF16)


def mm(a, b):
    return lax.dot_general(a, b, (((1,), (0,)), ((), ())), preferred_element_type=F32)


def mm_f32(a, b, dims=((1,), (0,))):
    return lax.dot_general(
        a, b, (dims, ((), ())), precision=lax.Precision.HIGHEST, preferred_element_type=F32
    )


def keep_lanes(ref, start, value):
    rows, width = value.shape
    for c in range(width // 128):
        ref[c, start : start + rows, :] = value[:, c * 128 : (c + 1) * 128]


def every_nth(ref, start, count, stride):
    return jnp.concatenate(
        [ref[c, pl.ds(start, count, stride=stride), :] for c in range(ref.shape[0])], axis=1)


def row_up(field, edge, index):
    rows = field.shape[0]
    return jnp.where(index == rows - 1, edge, pltpu.roll(field, rows - 1, 0))


def row_down(field, edge, index):
    return jnp.where(index == 0, edge, pltpu.roll(field, 1, 0))


def wave_twice(h, u, v, low, high, velocities):
    rows = h.shape[0]
    index = lax.broadcasted_iota(jnp.int32, h.shape, 0)
    u_low, q_low, r_low, s_low = low
    u_high, q_high, r_high, s_high = high
    h1 = h - HALF * (row_up(u, u_high, index) - row_down(u, u_low, index)) - COURANT * d_y(v)
    h1_low = q_low - HALF * u[0:1]
    h1_high = q_high + HALF * u[rows - 1 : rows]
    u1 = u - HALF * (row_up(h1, h1_high, index) - row_down(h1, h1_low, index)) + ROTATION * v
    v1 = v - COURANT * d_y(h1) - ROTATION * u
    u1_low = r_low - HALF * h1[0:1]
    u1_high = r_high + HALF * h1[rows - 1 : rows]
    h2 = h1 - HALF * (row_up(u1, u1_high, index) - row_down(u1, u1_low, index)) - COURANT * d_y(v1)
    if not velocities:
        return h2
    keep = 1.0 - HALF * HALF
    square = COURANT * COURANT
    h2_low = keep * h1_low + square * d_y(d_y(h1_low)) + s_low - HALF * u1[0:1]
    h2_high = keep * h1_high + square * d_y(d_y(h1_high)) + s_high + HALF * u1[rows - 1 : rows]
    u2 = u1 - HALF * (row_up(h2, h2_high, index) - row_down(h2, h2_low, index)) + ROTATION * v1
    v2 = v1 - COURANT * d_y(h2) - ROTATION * u1
    return h2, u2, v2


def edge_rows(h, u, v, sign):
    a = sign * HALF
    dv0 = COURANT * d_y(v[0])
    q = h[0] + a * u[1] - dv0
    h1_1 = h[1] - a * (u[0] - u[2]) - COURANT * d_y(v[1])
    r = u[0] + a * h1_1 + ROTATION * v[0]
    h1_2 = h[2] - a * (u[1] - u[3]) - COURANT * d_y(v[2])
    p = u[1] + a * h1_2 + ROTATION * v[1]
    s = a * p - dv0 + COURANT * ROTATION * d_y(u[0])
    h1 = a * u[0]
    first = (1.0 - 2.0 * HALF * HALF) * h1 + a * r + COURANT * COURANT * d_y(d_y(h1))
    return (u[0], q, r, s), (first, HALF * HALF * q, HALF * HALF * h1)


def edges_kernel(members, cells_x, x_ref, low_ref, high_ref, added_ref, lanes_ref):
    keep_lanes(lanes_ref, 0, x_ref[...])

    def across(field, row):
        return every_nth(lanes_ref, field * cells_x + row, members, 3 * cells_x)

    last = cells_x - 1
    for side, (out_ref, sign) in enumerate(((low_ref, 1.0), (high_ref, -1.0))):
        rows = [last - i if sign > 0 else i for i in range(4)]
        sent, added = edge_rows(
            [across(0, i) for i in rows[:3]], [across(1, i) for i in rows],
            [across(2, i) for i in rows[:3]], sign)
        for i in range(4):
            out_ref[pl.ds(i * members, members), :] = sent[i]
        for i in range(3):
            added_ref[pl.ds((3 * side + i) * members, members), :] = added[i]


def prior_kernel(members, cells_x, slabs, batches, me_ref, owner_ref, x_ref, added_ref, offset_ref,
                 obs_ref, rows_ref):
    cells_y = x_ref.shape[1]
    nobs = offset_ref.shape[1]
    zero = (jnp.zeros((1, cells_y), F32),) * 4
    base = members * cells_x
    for m in range(members):
        start = m * 3 * cells_x
        h, u, v = (x_ref[pl.ds(start + f * cells_x, cells_x), :] for f in range(3))
        rows_ref[pl.ds(m * cells_x, cells_x), :] = wave_twice(h, u, v, zero, zero, False)
    rows_ref[pl.ds(base, 6 * members), :] = added_ref[...]

    values = rows_ref[...]
    part0 = values.astype(BF16)
    rest = values - part0.astype(F32)
    part1 = rest.astype(BF16)
    part2 = (rest - part1.astype(F32)).astype(BF16)
    me = me_ref[0]
    total = cells_x * slabs
    for b in range(batches):
        offset = offset_ref[b : b + 1, :]
        column = lax.rem(offset, cells_y)
        row = lax.div(offset, cells_y)
        relative = row + lax.rem(owner_ref[b % slabs] - me + slabs, slabs) * cells_x
        pick = jnp.where(
            lax.broadcasted_iota(jnp.int32, (cells_y, nobs), 0) == column, 1.0, 0.0).astype(BF16)
        found = mm(part0, pick) + (mm(part1, pick) + mm(part2, pick))
        inside = lax.broadcasted_iota(jnp.int32, (cells_x, nobs), 0) == relative
        edges = jnp.zeros((members, nobs), F32)
        for i in range(3):
            piece = found[base + i * members : base + (i + 1) * members]
            edges += jnp.where(relative == cells_x + i, piece, 0.0)
            piece = found[base + (3 + i) * members : base + (4 + i) * members]
            edges += jnp.where(relative == total - 1 - i, piece, 0.0)
        own = [
            jnp.sum(jnp.where(inside, found[m * cells_x : (m + 1) * cells_x], 0.0),
                    axis=0, keepdims=True)
            for m in range(members)
        ]
        obs_ref[:, b * nobs : (b + 1) * nobs] = jnp.concatenate(own, axis=0) + edges


def forecast_kernel(members, cells_x, x_ref, low_ref, high_ref, out_ref, rows_ref):
    cells_y = x_ref.shape[1]
    chunk = out_ref.shape[2]
    piece = math.gcd(chunk, cells_y)
    for m in range(members):
        start = m * 3 * cells_x
        h, u, v = (x_ref[pl.ds(start + f * cells_x, cells_x), :] for f in range(3))
        low = [low_ref[pl.ds(i * members + m, 1), :] for i in range(4)]
        high = [high_ref[pl.ds(i * members + m, 1), :] for i in range(4)]
        for f, value in enumerate(wave_twice(h, u, v, low, high, True)):
            keep_lanes(rows_ref, start + f * cells_x, value)
    for r in range(cells_x):
        for f in range(3):
            line = every_nth(rows_ref, f * cells_x + r, members, 3 * cells_x)
            for c in range(0, cells_y, piece):
                flat = (r * 3 + f) * cells_y + c
                out_ref[flat // chunk, :, flat % chunk : flat % chunk + piece] = line[:, c : c + piece]


def column_of(row):
    return jnp.transpose(jnp.broadcast_to(row, (8,) + row.shape[1:]))[:, 0:1]


def taper_of(row_i, column_i, inverse_i, row_j, column_j, total_x, cells_y):
    gap_x = jnp.abs(row_j - row_i)
    gap_x = jnp.minimum(gap_x, total_x - gap_x)
    gap_y = jnp.abs(column_j - column_i)
    gap_y = jnp.minimum(gap_y, cells_y - gap_y)
    distance = jnp.sqrt(gap_x * gap_x + gap_y * gap_y)
    ramp = jnp.maximum(0.0, 1.0 - distance * inverse_i)
    return ramp * ramp


def geometry(owner_ref, offset_ref, cutoff_ref, b, slabs, cells_x, cells_y):
    offset = offset_ref[b : b + 1, :]
    row = lax.div(offset, cells_y) + owner_ref[b % slabs] * cells_x
    column = lax.rem(offset, cells_y)
    return row.astype(F32), column.astype(F32), 1.0 / cutoff_ref[b : b + 1, :].astype(F32)


def taper_kernel(slabs, cells_x, cells_y, batches, tile, groups, first_ref, owner_ref, offset_ref,
                 cutoff_ref, out_ref):
    for b in range(batches):
        row, column, inverse = geometry(owner_ref, offset_ref, cutoff_ref, b, slabs, cells_x, cells_y)
        row, column, inverse = column_of(row), column_of(column), column_of(inverse)
        for g, at in enumerate(groups):
            start = first_ref[0] + at
            cell_row = lax.div(start, 3 * cells_y).astype(F32)
            cell_column = (lax.rem(start, cells_y) + lax.broadcasted_iota(jnp.int32, (1, tile), 1)).astype(F32)
            out_ref[b, g] = taper_of(row, column, inverse, cell_row, cell_column,
                                     float(cells_x * slabs), float(cells_y))


def solve_members(gram, right, lowest, work_ref):
    size = gram.shape[0]
    top = jnp.max(jnp.sum(jnp.abs(gram), axis=1, keepdims=True), axis=0, keepdims=True)
    top = jnp.maximum(top, 4.0 * lowest)
    eye = jnp.where(
        lax.broadcasted_iota(jnp.int32, (size, size), 0)
        == lax.broadcasted_iota(jnp.int32, (size, size), 1), 1.0, 0.0)
    alpha = 2.0 / (top + lowest)

    def double(r, x, t):
        t = 2.0 * t * t - 1.0
        extra = 1.0 / t
        both = mm_f32(r, jnp.concatenate([r, x], axis=1))
        gain = 1.0 + extra
        return gain * both[:, :size] - extra * eye, gain * (x + both[:, size:]), t

    r, x, t = eye - alpha * gram, alpha * right, (top + lowest) / (top - lowest)
    for _ in range(ROUNDS):
        r, x, t = double(r, x, t)
    work_ref[:, :size] = r
    work_ref[:, size:] = x

    def more(t):
        r, x, t = double(work_ref[:, :size], work_ref[:, size:], jnp.full((1, 1), t, F32))
        work_ref[:, :size] = r
        work_ref[:, size:] = x
        return t[0, 0]

    lax.while_loop(lambda t: t < CONVERGED, more, t[0, 0])
    return work_ref[:, size:]


def chain_kernel(slabs, cells_x, cells_y, batches, parts, *refs):
    place_ref, owner_ref, offset_ref, cutoff_ref, values_ref, variance_ref, perturb_ref = refs[:7]
    part_refs = refs[7 : 7 + parts]
    y_ref, w_ref, obs_ref, work_ref = refs[7 + parts :]
    members = obs_ref.shape[0]
    nobs = offset_ref.shape[1]
    each = part_refs[0].shape[0]
    scale = 1.0 / (members - 1)
    for k in range(parts):
        obs_ref[pl.ds(pl.multiple_of(place_ref[k] * each, each), each), :] = part_refs[k][...]
    eye = (lax.broadcasted_iota(jnp.int32, (members, members), 0)
           == lax.broadcasted_iota(jnp.int32, (members, members), 1))
    places = [geometry(owner_ref, offset_ref, cutoff_ref, b, slabs, cells_x, cells_y)
              for b in range(batches)]
    for b in range(batches):
        observed = obs_ref[:, b * nobs : (b + 1) * nobs]
        spread = observed - jnp.mean(observed, axis=0, keepdims=True)
        variance = variance_ref[b : b + 1, :]
        inverse = 1.0 / variance
        target = values_ref[b : b + 1, :] + jnp.sqrt(variance) * perturb_ref[b] - observed
        both = mm_f32(spread * inverse, jnp.concatenate([spread, target], axis=0), ((1,), (1,)))
        gram = both[:, :members] + jnp.where(eye, float(members - 1), 0.0)
        solved = solve_members(gram, both[:, members:], float(members - 1), work_ref)
        weights = (target - mm_f32(solved, spread, ((0,), (0,)))) * inverse
        spread_t = jnp.transpose(spread) * scale
        high, low = split2(spread_t)
        y_ref[b] = jnp.concatenate([high, high, low], axis=1)
        high, low = split2(weights)
        w_ref[b] = jnp.concatenate([high, low], axis=0)
        if b + 1 < batches:
            later = obs_ref[:, (b + 1) * nobs :]
            anomaly = later - jnp.mean(later, axis=0, keepdims=True)
            covariance = mm_f32(spread_t, anomaly)
            row, column, inverse_cutoff = (column_of(x) for x in places[b])
            row_j = jnp.concatenate([places[c][0] for c in range(b + 1, batches)], axis=1)
            column_j = jnp.concatenate([places[c][1] for c in range(b + 1, batches)], axis=1)
            taper = taper_of(row, column, inverse_cutoff, row_j, column_j,
                             float(cells_x * slabs), float(cells_y))
            obs_ref[:, (b + 1) * nobs :] = later + mm_f32(weights, covariance * taper)


def update_kernel(batches, tile, groups, s_ref, y_ref, w_ref, taper_ref, out_ref):
    members = s_ref.shape[0]
    for g, tiles in enumerate(groups):
        state = jnp.concatenate([s_ref[:, at : at + tile] for at in tiles], axis=1)
        for b in range(batches):
            anomaly = state - jnp.mean(state, axis=0, keepdims=True)
            high, low = split2(anomaly)
            covariance = mm(y_ref[b], jnp.concatenate([high, low, high], axis=0))
            taper = taper_ref[b, g]
            gain = covariance * jnp.concatenate([taper] * len(tiles), axis=1)
            high, low = split2(gain)
            two = mm(w_ref[b], high)
            one = mm(w_ref[b, :members], low)
            state = state + (two[:members] + (two[members:] + one))
        for i, at in enumerate(tiles):
            out_ref[:, at : at + tile] = state[:, i * tile : (i + 1) * tile]


def on_device(prior, obs_values, obs_variance, obs_perturb, obs_offset, owner_order, taper_cutoff):
    slabs = lax.axis_size("slab")
    shards = lax.axis_size("member")
    each, cells_x, _, cells_y = prior.shape
    batches, nobs = obs_values.shape
    members = each * shards
    chunk = 3 * cells_x * cells_y // shards
    slab = lax.axis_index("slab")
    member = lax.axis_index("member")
    x = prior.transpose(0, 2, 1, 3).reshape(each * 3 * cells_x, cells_y)
    owner = owner_order.astype(jnp.int32)
    perturb = obs_perturb.transpose(0, 2, 1)

    def shift(count, by):
        return [(i, (i + by) % count) for i in range(count)]

    def permute(array, axis, count, by):
        return lax.ppermute(array, axis, shift(count, by))

    edge = jax.ShapeDtypeStruct((4 * each, cells_y), F32)
    low, high, added = pl.pallas_call(
        functools.partial(edges_kernel, each, cells_x),
        out_shape=(edge, edge, jax.ShapeDtypeStruct((6 * each, cells_y), F32)),
        in_specs=[VMEM_SPEC],
        out_specs=(VMEM_SPEC,) * 3,
        scratch_shapes=[pltpu.VMEM((cells_y // 128, each * 3 * cells_x, 128), F32)],
        name="edges",
    )(x)
    low = lax.ppermute(low, "slab", shift(slabs, 1))
    high = lax.ppermute(high, "slab", shift(slabs, -1))

    partial = pl.pallas_call(
        functools.partial(prior_kernel, each, cells_x, slabs, batches),
        out_shape=jax.ShapeDtypeStruct((each, batches * nobs), F32),
        in_specs=[SMEM_SPEC, SMEM_SPEC, VMEM_SPEC, VMEM_SPEC, VMEM_SPEC],
        out_specs=VMEM_SPEC,
        scratch_shapes=[pltpu.VMEM((each * cells_x + 6 * each, cells_y), F32)],
        name="prior",
    )(slab.reshape(1), owner, x, added, obs_offset)

    observed = partial
    for by in range(1, slabs):
        observed = observed + permute(partial, "slab", slabs, by)
    pieces = [observed]
    for by in range(1, shards):
        pieces.append(permute(observed, "member", shards, by))
    place = lax.rem(member - jnp.arange(shards, dtype=jnp.int32) + shards, shards)

    outgoing = pl.pallas_call(
        functools.partial(forecast_kernel, each, cells_x),
        out_shape=jax.ShapeDtypeStruct((shards, each, chunk), F32),
        in_specs=[VMEM_SPEC] * 3,
        out_specs=VMEM_SPEC,
        scratch_shapes=[pltpu.VMEM((cells_y // 128, each * 3 * cells_x, 128), F32)],
        name="forecast",
    )(x, low, high)
    state = lax.all_to_all(outgoing, "member", 0, 0).reshape(members, chunk)

    tile = math.gcd(chunk, 256)
    if chunk % (3 * cells_y) == 0:
        groups = [
            [r * 3 * cells_y + f * cells_y + c for f in range(3)]
            for r in range(chunk // (3 * cells_y))
            for c in range(0, cells_y, tile)
        ]
    else:
        groups = [[at] for at in range(0, chunk, tile)]
    first = (slab * shards + member) * chunk
    taper = pl.pallas_call(
        functools.partial(
            taper_kernel, slabs, cells_x, cells_y, batches, tile, [g[0] for g in groups]),
        out_shape=jax.ShapeDtypeStruct((batches, len(groups), nobs, tile), F32),
        in_specs=[SMEM_SPEC, SMEM_SPEC, VMEM_SPEC, VMEM_SPEC],
        out_specs=VMEM_SPEC,
        name="taper",
    )(first.reshape(1), owner, obs_offset, taper_cutoff)

    chain = pl.pallas_call(
        functools.partial(chain_kernel, slabs, cells_x, cells_y, batches, shards),
        out_shape=(
            jax.ShapeDtypeStruct((batches, nobs, 3 * members), BF16),
            jax.ShapeDtypeStruct((batches, 2 * members, nobs), BF16),
        ),
        in_specs=[SMEM_SPEC, SMEM_SPEC] + [VMEM_SPEC] * (5 + shards),
        out_specs=(VMEM_SPEC,) * 2,
        scratch_shapes=[
            pltpu.VMEM((members, batches * nobs), F32),
            pltpu.VMEM((members, 2 * members), F32),
        ],
        name="chain",
    )
    y_all, w_all = chain(
        place, owner, obs_offset, taper_cutoff, obs_values, obs_variance, perturb, *pieces)

    return pl.pallas_call(
        functools.partial(update_kernel, batches, tile, groups),
        out_shape=jax.ShapeDtypeStruct((members, chunk), F32),
        in_specs=[VMEM_SPEC] * 4,
        out_specs=VMEM_SPEC,
        name="update",
    )(state, y_all, w_all, taper)


def solution(mesh):
    in_specs = (P("member", "slab", None, None), P(), P(), P(), P(), P(), P())
    out_specs = P(None, ("slab", "member"))

    return jax.shard_map(on_device, mesh=mesh, in_specs=in_specs, out_specs=out_specs, check_vma=False)
```

```python
import functools
import math

import jax
import jax.numpy as jnp
from jax import lax
from jax.experimental import pallas as pl
from jax.experimental.pallas import tpu as pltpu
from jax.sharding import PartitionSpec as P


COURANT = 0.3
ROTATION = 0.1
HALF = COURANT * 0.5
ROUNDS = 6
TINY = 1e-30
CONVERGED = 1e6
F32 = jnp.float32
BF16 = jnp.bfloat16
VMEM_SPEC = pl.BlockSpec(memory_space=pltpu.VMEM)
ANY_SPEC = pl.BlockSpec(memory_space=pl.ANY)
SMEM_SPEC = pl.BlockSpec(memory_space=pltpu.SMEM)


def d_y(field, scale=1.0):
    width = field.shape[-1]
    axis = field.ndim - 1
    return (pltpu.roll(field, width - 1, axis) - pltpu.roll(field, 1, axis)) * (0.5 * scale)


def split2(x):
    high = x.astype(BF16)
    return high, (x - high.astype(F32)).astype(BF16)


def mm(a, b):
    return lax.dot_general(a, b, (((1,), (0,)), ((), ())), preferred_element_type=F32)


def mm_f32(a, b, dims=((1,), (0,))):
    return lax.dot_general(
        a, b, (dims, ((), ())), precision=lax.Precision.HIGHEST, preferred_element_type=F32
    )


def keep_lanes(ref, start, value):
    rows, width = value.shape
    for c in range(width // 128):
        ref[c, start : start + rows, :] = value[:, c * 128 : (c + 1) * 128]


def every_nth(ref, start, count, stride):
    return jnp.concatenate(
        [ref[c, pl.ds(start, count, stride=stride), :] for c in range(ref.shape[0])], axis=1)


def row_up(field, edge, index):
    rows = field.shape[0]
    return jnp.where(index == rows - 1, edge, pltpu.roll(field, rows - 1, 0))


def row_down(field, edge, index):
    return jnp.where(index == 0, edge, pltpu.roll(field, 1, 0))


def wave_heights(h, u, v):
    rows = h.shape[0]
    index = lax.broadcasted_iota(jnp.int32, h.shape, 0)
    h1 = h - HALF * (row_up(u, 0.0, index) - row_down(u, 0.0, index)) - d_y(v, COURANT)
    below, above = -HALF * u[0:1], HALF * u[rows - 1 : rows]
    u1 = u - HALF * (row_up(h1, above, index) - row_down(h1, below, index)) + ROTATION * v
    v1 = v - d_y(h1, COURANT) - ROTATION * u
    below, above = -HALF * h1[0:1], HALF * h1[rows - 1 : rows]
    h2 = h1 - HALF * (row_up(u1, above, index) - row_down(u1, below, index)) - d_y(v1, COURANT)
    return h2, u1, v1


def edge_rows(h, u, v, sign):
    a = sign * HALF
    dv0 = COURANT * d_y(v[0])
    q = h[0] + a * u[1] - dv0
    h1_1 = h[1] - a * (u[0] - u[2]) - COURANT * d_y(v[1])
    r = u[0] + a * h1_1 + ROTATION * v[0]
    h1_2 = h[2] - a * (u[1] - u[3]) - COURANT * d_y(v[2])
    p = u[1] + a * h1_2 + ROTATION * v[1]
    s = a * p - dv0 + COURANT * ROTATION * d_y(u[0])
    h1 = a * u[0]
    first = (1.0 - 2.0 * HALF * HALF) * h1 + a * r + COURANT * COURANT * d_y(d_y(h1))
    return (u[0], q, r, s), (first, HALF * HALF * q, HALF * HALF * h1)


def prior_kernel(members, cells_x, slabs, batches, me_ref, owner_ref, x_ref, offset_ref,
                 obs_ref, next_ref, prev_ref, mid_ref, rim_ref, rows_ref, lanes_ref):
    cells_y = x_ref.shape[1]
    nobs = offset_ref.shape[1]
    base = members * cells_x
    for m in range(members):
        start = m * 3 * cells_x
        fields = [x_ref[pl.ds(start + f * cells_x, cells_x), :] for f in range(3)]
        after = wave_heights(*fields)
        rows_ref[pl.ds(m * cells_x, cells_x), :] = after[0]
        for f in range(3):
            keep_lanes(lanes_ref, start + f * cells_x, fields[f])
            keep_lanes(mid_ref, start + f * cells_x, after[f])

    def across(field, row):
        return every_nth(lanes_ref, field * cells_x + row, members, 3 * cells_x)

    last = cells_x - 1
    for side, (out_ref, sign) in enumerate(((next_ref, 1.0), (prev_ref, -1.0))):
        rows = [last - i if sign > 0 else i for i in range(4)]
        sent, added = edge_rows(
            [across(0, i) for i in rows[:3]], [across(1, i) for i in rows],
            [across(2, i) for i in rows[:3]], sign)
        for i in range(4):
            out_ref[pl.ds(i * members, members), :] = sent[i]
        for i in range(3):
            rows_ref[pl.ds(base + (3 * side + i) * members, members), :] = added[i]
        rim_ref[pl.ds((1 - side) * members, members), :] = sent[0]

    values = rows_ref[...]
    part0 = values.astype(BF16)
    rest = values - part0.astype(F32)
    part1 = rest.astype(BF16)
    part2 = (rest - part1.astype(F32)).astype(BF16)
    me = me_ref[0]
    total = cells_x * slabs
    for b in range(batches):
        offset = offset_ref[b : b + 1, :]
        column = lax.rem(offset, cells_y)
        row = lax.div(offset, cells_y)
        relative = row + lax.rem(owner_ref[b % slabs] - me + slabs, slabs) * cells_x
        pick = jnp.where(
            lax.broadcasted_iota(jnp.int32, (cells_y, nobs), 0) == column, 1.0, 0.0).astype(BF16)
        found = mm(part0, pick) + (mm(part1, pick) + mm(part2, pick))
        inside = lax.broadcasted_iota(jnp.int32, (cells_x, nobs), 0) == relative
        edges = jnp.zeros((members, nobs), F32)
        for i in range(3):
            piece = found[base + i * members : base + (i + 1) * members]
            edges += jnp.where(relative == cells_x + i, piece, 0.0)
            piece = found[base + (3 + i) * members : base + (4 + i) * members]
            edges += jnp.where(relative == total - 1 - i, piece, 0.0)
        own = [
            jnp.sum(jnp.where(inside, found[m * cells_x : (m + 1) * cells_x], 0.0),
                    axis=0, keepdims=True)
            for m in range(members)
        ]
        whole = jnp.concatenate(own, axis=0) + edges
        at = b * nobs
        place = (pl.ds(at // cells_y * members, members), slice(at % cells_y, at % cells_y + nobs))
        obs_ref[place] = whole
        for out_ref in (next_ref, prev_ref):
            out_ref[pl.ds(4 * members + at // cells_y * members, members), place[1]] = whole


def spot(chunk, cells_y, row, field, column):
    return divmod((row * 3 + field) * cells_y + column, chunk)


def forecast_kernel(members, cells_x, mid_ref, rim_ref, out_ref, rows_ref):
    cells_y = rim_ref.shape[1]
    chunk = out_ref.shape[2]
    piece = math.gcd(chunk, cells_y)
    tiles = range(cells_y // 128)
    index = lax.broadcasted_iota(jnp.int32, (cells_x, cells_y), 0)
    for m in range(members):
        start = m * 3 * cells_x
        h2, u1, v1 = (
            jnp.concatenate([mid_ref[c, start + f * cells_x : start + (f + 1) * cells_x, :] for c in tiles], axis=1)
            for f in range(3))
        u2 = u1 - HALF * (row_up(h2, 0.0, index) - row_down(h2, 0.0, index)) + ROTATION * v1
        v2 = v1 - d_y(h2, COURANT) - ROTATION * u1
        keep_lanes(rows_ref, m * 2 * cells_x, u2)
        keep_lanes(rows_ref, (m * 2 + 1) * cells_x, v2)

    def rim_height(side, sign):
        u = rim_ref[pl.ds(side * members, members), :]
        u1 = every_nth(mid_ref, cells_x + (cells_x - 1) * side, members, 3 * cells_x)
        return sign * HALF * ((1.0 - HALF * HALF) * u + COURANT * COURANT * d_y(d_y(u)) + u1)

    outside = {(0, 1): HALF * rim_height(0, -1.0), (cells_x - 1, 1): -HALF * rim_height(1, 1.0)}
    for r in range(cells_x):
        for f in range(3):
            if f == 0:
                line = every_nth(mid_ref, r, members, 3 * cells_x)
            else:
                line = every_nth(rows_ref, (f - 1) * cells_x + r, members, 2 * cells_x)
            if (r, f) in outside:
                line = line + outside[r, f]
            for c in range(0, cells_y, piece):
                dest, lane = spot(chunk, cells_y, r, f, c)
                out_ref[dest, :, lane : lane + piece] = line[:, c : c + piece]


def edge_forecast(message, members, sign):
    a = sign * HALF
    u, q, r, s = (message[i * members : (i + 1) * members] for i in range(4))
    square = COURANT * COURANT
    h1 = a * u
    u1_0, u1_1 = a * q, a * h1
    v1 = -d_y(h1, COURANT)
    h2_0 = (1.0 - 2.0 * a * a) * h1 + a * r + square * d_y(d_y(h1))
    h2_1, h2_2 = a * u1_0, a * u1_1
    h2_edge = (1.0 - 2.0 * a * a) * q + square * d_y(d_y(q)) + s
    return {
        (0, 0): h2_0, (1, 0): h2_1, (2, 0): h2_2,
        (0, 1): u1_0 - a * (h2_1 - h2_edge) + ROTATION * v1,
        (1, 1): u1_1 - a * (h2_2 - h2_0), (2, 1): a * h2_1, (3, 1): a * h2_2,
        (0, 2): v1 - COURANT * d_y(h2_0) - ROTATION * u1_0,
        (1, 2): -COURANT * d_y(h2_1) - ROTATION * u1_1, (2, 2): -COURANT * d_y(h2_2),
    }


def correct_kernel(members, cells_x, others, *refs):
    low_ref, high_ref, partial_ref = refs[:3]
    other_refs, in_ref = refs[3 : 3 + others], refs[3 + others]
    out_ref, sum_ref, message_ref, obs_ref, block_ref, in_sems, out_sems = refs[4 + others :]
    cells_y = sum_ref.shape[1]
    shards, _, chunk = in_ref.shape
    touched = block_ref.shape[1]
    piece = math.gcd(chunk, cells_y)
    spans = [pl.ds(0, touched), pl.ds(shards - touched, touched)]
    moves = [(low_ref, message_ref.at[0]), (high_ref, message_ref.at[1]), (partial_ref, obs_ref.at[0])]
    moves += [(ref, obs_ref.at[1 + i]) for i, ref in enumerate(other_refs)]
    moves += [(in_ref.at[spans[i]], block_ref.at[i]) for i in range(2)]
    copies = [pltpu.make_async_copy(a, b, in_sems.at[i]) for i, (a, b) in enumerate(moves)]
    for copy in copies:
        copy.start()
    for copy in copies:
        copy.wait()
    total = message_ref[0, 4 * members :, :] + message_ref[1, 4 * members :, :]
    for i in range(1 + others):
        total = total + obs_ref[i]
    sum_ref[...] = total
    written = []
    for side, sign in ((0, 1.0), (1, -1.0)):
        message = message_ref[side, : 4 * members, :]
        for (i, f), value in edge_forecast(message, members, sign).items():
            row = i if sign > 0 else cells_x - 1 - i
            for c in range(0, cells_y, piece):
                dest, lane = spot(chunk, cells_y, row, f, c)
                at = (side, dest - side * (shards - touched), slice(None), slice(lane, lane + piece))
                block_ref[at] = block_ref[at] + value[:, c : c + piece]
        written.append(pltpu.make_async_copy(block_ref.at[side], out_ref.at[spans[side]], out_sems.at[side]))
        written[-1].start()
    for copy in written:
        copy.wait()


def column_of(row, lanes=128):
    return jnp.transpose(jnp.broadcast_to(row, (lanes,) + row.shape[1:]))


def gap2(a, b, around, inverse):
    gap = jnp.abs(a - b)
    gap = jnp.minimum(gap, around - gap) * inverse
    return gap * gap


def taper_of(squared):
    ramp = jnp.maximum(0.0, 1.0 - squared * lax.rsqrt(squared))
    return ramp * ramp


def geometry(owner_ref, offset_ref, cutoff_ref, b, slabs, cells_x, cells_y):
    offset = offset_ref[b : b + 1, :]
    row = lax.div(offset, cells_y) + owner_ref[b % slabs] * cells_x
    column = lax.rem(offset, cells_y)
    return row.astype(F32), column.astype(F32), 1.0 / cutoff_ref[b : b + 1, :].astype(F32)


def taper_kernel(slabs, cells_x, cells_y, batches, tile, groups, first_ref, owner_ref, offset_ref,
                 cutoff_ref, out_ref):
    starts = [first_ref[0] + at for at in groups]
    columns = {}
    for g, at in enumerate(groups):
        columns.setdefault(at % cells_y, []).append(g)
    for b in range(batches):
        row, column, inverse = (
            column_of(x) for x in geometry(owner_ref, offset_ref, cutoff_ref, b, slabs, cells_x, cells_y))
        rows = [gap2(lax.div(start, 3 * cells_y).astype(F32), row, float(cells_x * slabs), inverse)
                for start in starts]
        for members in columns.values():
            for lane in range(0, tile, 128):
                cell = (lax.rem(starts[members[0]], cells_y) + lane
                        + lax.broadcasted_iota(jnp.int32, (1, 128), 1)).astype(F32)
                gap_y = jnp.maximum(gap2(cell, column, float(cells_y), inverse), TINY)
                for g in members:
                    out_ref[g, b, :, lane : lane + 128] = taper_of(gap_y + rows[g])


def solve_members(gram, right, lowest, work_ref):
    size = gram.shape[0]
    top = jnp.max(jnp.sum(jnp.abs(gram), axis=1, keepdims=True), axis=0, keepdims=True)
    top = jnp.maximum(top, 4.0 * lowest)
    eye = jnp.where(
        lax.broadcasted_iota(jnp.int32, (size, size), 0)
        == lax.broadcasted_iota(jnp.int32, (size, size), 1), 1.0, 0.0)
    alpha = 2.0 / (top + lowest)

    def double(r, x, t):
        t = 2.0 * t * t - 1.0
        extra = 1.0 / t
        both = mm_f32(r, jnp.concatenate([r, x], axis=1))
        gain = 1.0 + extra
        return gain * both[:, :size] - extra * eye, gain * (x + both[:, size:]), t

    r, x, t = eye - alpha * gram, alpha * right, (top + lowest) / (top - lowest)
    for _ in range(ROUNDS):
        r, x, t = double(r, x, t)
    work_ref[:, :size] = r
    work_ref[:, size:] = x

    def more(t):
        r, x, t = double(work_ref[:, :size], work_ref[:, size:], jnp.full((1, 1), t, F32))
        work_ref[:, :size] = r
        work_ref[:, size:] = x
        return t[0, 0]

    lax.while_loop(lambda t: t < CONVERGED, more, t[0, 0])
    return work_ref[:, size:]


def stack3(state):
    high, low = split2(state - jnp.mean(state, axis=0, keepdims=True))
    return jnp.concatenate([high, low, high], axis=0)


def weigh(pair, high, low):
    members = pair.shape[0] // 2
    main, rest = mm(pair, high), mm(pair, low)
    return main[:members] + (main[members:] + rest[:members])


def chain_kernel(slabs, cells_x, cells_y, batches, parts, *refs):
    place_ref, owner_ref, offset_ref, cutoff_ref, values_ref, variance_ref, perturb_ref = refs[:7]
    part_refs = refs[7 : 7 + parts]
    y_ref, w_ref, obs_ref, work_ref = refs[7 + parts :]
    members = obs_ref.shape[0]
    nobs = offset_ref.shape[1]
    each = part_refs[0].shape[0]
    scale = 1.0 / (members - 1)
    each = each * cells_y // obs_ref.shape[1]
    for k in range(parts):
        at = pl.ds(pl.multiple_of(place_ref[k] * each, each), each)
        for c in range(obs_ref.shape[1] // cells_y):
            obs_ref[at, c * cells_y : (c + 1) * cells_y] = part_refs[k][c * each : (c + 1) * each, :]
    eye = (lax.broadcasted_iota(jnp.int32, (members, members), 0)
           == lax.broadcasted_iota(jnp.int32, (members, members), 1))
    places = [geometry(owner_ref, offset_ref, cutoff_ref, b, slabs, cells_x, cells_y)
              for b in range(batches)]
    for b in range(batches):
        observed = obs_ref[:, b * nobs : (b + 1) * nobs]
        spread = observed - jnp.mean(observed, axis=0, keepdims=True)
        variance = variance_ref[b : b + 1, :]
        inverse = 1.0 / variance
        target = values_ref[b : b + 1, :] + jnp.sqrt(variance) * perturb_ref[b] - observed
        both = mm_f32(spread * inverse, jnp.concatenate([spread, target], axis=0), ((1,), (1,)))
        gram = both[:, :members] + jnp.where(eye, float(members - 1), 0.0)
        high, low = split2(jnp.transpose(spread) * scale)
        spread_t = jnp.concatenate([high, high, low], axis=1)
        y_ref[b] = spread_t
        if b + 1 < batches:
            later = obs_ref[:, (b + 1) * nobs :]
            row, column, inverse_cutoff = (column_of(x) for x in places[b])
            tapers = []
            for c in range(b + 1, batches):
                for lane in range(0, nobs, 128):
                    row_j, column_j = (x[:, lane : lane + 128] for x in places[c][:2])
                    squared = (gap2(row_j, row, float(cells_x * slabs), inverse_cutoff)
                               + gap2(column_j, column, float(cells_y), inverse_cutoff))
                    tapers.append(taper_of(jnp.maximum(squared, TINY)))
            gain_high, gain_low = split2(
                mm(spread_t, stack3(later)) * jnp.concatenate(tapers, axis=1))
        solved = solve_members(gram, both[:, members:], float(members - 1), work_ref)
        weights = (target - mm_f32(solved, spread, ((0,), (0,)))) * inverse
        high, low = split2(weights)
        pair = jnp.concatenate([high, low], axis=0)
        w_ref[b] = pair
        if b + 1 < batches:
            obs_ref[:, (b + 1) * nobs :] = later + weigh(pair, gain_high, gain_low)


def update_kernel(batches, tile, groups, s_ref, y_ref, w_ref, taper_ref, out_ref):
    for b in range(batches):
        for g, tiles in enumerate(groups):
            for at in tiles:
                state = (out_ref if b else s_ref)[:, at : at + tile]
                covariance = mm(y_ref[b], stack3(state))
                high, low = split2(covariance * taper_ref[g, b])
                out_ref[:, at : at + tile] = state + weigh(w_ref[b], high, low)


def on_device(prior, obs_values, obs_variance, obs_perturb, obs_offset, owner_order, taper_cutoff):
    slabs = lax.axis_size("slab")
    shards = lax.axis_size("member")
    each, cells_x, _, cells_y = prior.shape
    batches, nobs = obs_values.shape
    members = each * shards
    chunk = 3 * cells_x * cells_y // shards
    slab = lax.axis_index("slab")
    member = lax.axis_index("member")
    x = prior.transpose(0, 2, 1, 3).reshape(each * 3 * cells_x, cells_y)
    owner = owner_order.astype(jnp.int32)
    perturb = obs_perturb.transpose(0, 2, 1)

    def shift(count, by):
        return [(i, (i + by) % count) for i in range(count)]

    lines = batches * nobs // cells_y * each
    message = jax.ShapeDtypeStruct((4 * each + lines, cells_y), F32)
    lane_tiles = (cells_y // 128, each * 3 * cells_x, 128)
    partial, to_next, to_prev, mid, rim = pl.pallas_call(
        functools.partial(prior_kernel, each, cells_x, slabs, batches),
        out_shape=(
            jax.ShapeDtypeStruct((lines, cells_y), F32), message, message,
            jax.ShapeDtypeStruct(lane_tiles, F32), jax.ShapeDtypeStruct((2 * each, cells_y), F32),
        ),
        in_specs=[SMEM_SPEC, SMEM_SPEC, VMEM_SPEC, VMEM_SPEC],
        out_specs=(VMEM_SPEC,) * 5,
        scratch_shapes=[
            pltpu.VMEM((each * cells_x + 6 * each, cells_y), F32),
            pltpu.VMEM(lane_tiles, F32),
        ],
        name="prior",
    )(slab.reshape(1), owner, x, obs_offset)
    low = lax.ppermute(to_next, "slab", shift(slabs, 1))
    high = lax.ppermute(to_prev, "slab", shift(slabs, -1))
    others = [lax.ppermute(partial, "slab", shift(slabs, by)) for by in range(2, slabs - 1)]

    outgoing = jax.ShapeDtypeStruct((shards, each, chunk), F32)
    inner = pl.pallas_call(
        functools.partial(forecast_kernel, each, cells_x),
        out_shape=outgoing,
        in_specs=[VMEM_SPEC] * 2,
        out_specs=VMEM_SPEC,
        scratch_shapes=[pltpu.VMEM((cells_y // 128, each * 2 * cells_x, 128), F32)],
        name="forecast",
    )(mid, rim)
    fixed = 3 + len(others)
    outgoing, observed = pl.pallas_call(
        functools.partial(correct_kernel, each, cells_x, len(others)),
        out_shape=(outgoing, jax.ShapeDtypeStruct((lines, cells_y), F32)),
        in_specs=[ANY_SPEC] * (fixed + 1),
        out_specs=(ANY_SPEC, VMEM_SPEC),
        input_output_aliases={fixed: 0},
        scratch_shapes=[
            pltpu.VMEM((2, 4 * each + lines, cells_y), F32),
            pltpu.VMEM((1 + len(others), lines, cells_y), F32),
            pltpu.VMEM((2, 4 * 3 * cells_y // chunk, each, chunk), F32),
            pltpu.SemaphoreType.DMA((fixed + 2,)),
            pltpu.SemaphoreType.DMA((2,)),
        ],
        name="correct",
    )(low, high, partial, *others, inner)

    pieces = [observed]
    for by in range(2, shards, 2):
        pieces.append(lax.ppermute(observed, "member", shift(shards, by)))
    swap = [(i, i ^ 1) for i in range(shards)]
    pieces += [lax.ppermute(p, "member", swap) for p in pieces]
    evens = jnp.arange(0, shards, 2, dtype=jnp.int32)
    place = lax.rem(jnp.concatenate([member - evens, (member ^ 1) - evens]) + shards, shards)

    state = lax.all_to_all(outgoing, "member", 0, 0).reshape(members, chunk)

    steps = max(1, chunk // (3 * cells_y))
    width = chunk // steps
    tile = math.gcd(width, 256)
    if width == 3 * cells_y:
        groups = [[f * cells_y + c for f in range(3)] for c in range(0, cells_y, tile)]
    else:
        groups = [[at] for at in range(0, width, tile)]
    firsts = [i * width + g[0] for i in range(steps) for g in groups]
    first = (slab * shards + member) * chunk
    taper = pl.pallas_call(
        functools.partial(
            taper_kernel, slabs, cells_x, cells_y, batches, tile, firsts),
        out_shape=jax.ShapeDtypeStruct((len(firsts), batches, nobs, tile), F32),
        in_specs=[SMEM_SPEC, SMEM_SPEC, VMEM_SPEC, VMEM_SPEC],
        out_specs=VMEM_SPEC,
        name="taper",
    )(first.reshape(1), owner, obs_offset, taper_cutoff)

    chain = pl.pallas_call(
        functools.partial(chain_kernel, slabs, cells_x, cells_y, batches, shards),
        out_shape=(
            jax.ShapeDtypeStruct((batches, nobs, 3 * members), BF16),
            jax.ShapeDtypeStruct((batches, 2 * members, nobs), BF16),
        ),
        in_specs=[SMEM_SPEC, SMEM_SPEC] + [VMEM_SPEC] * (5 + shards),
        out_specs=(VMEM_SPEC,) * 2,
        scratch_shapes=[
            pltpu.VMEM((members, batches * nobs), F32),
            pltpu.VMEM((members, 2 * members), F32),
        ],
        name="chain",
    )
    y_all, w_all = chain(
        place, owner, obs_offset, taper_cutoff, obs_values, obs_variance, perturb, *pieces)

    block = pl.BlockSpec((members, width), lambda i: (0, i))
    return pl.pallas_call(
        functools.partial(update_kernel, batches, tile, groups),
        grid=(steps,),
        out_shape=jax.ShapeDtypeStruct((members, chunk), F32),
        in_specs=[
            block, VMEM_SPEC, VMEM_SPEC,
            pl.BlockSpec((len(groups), batches, nobs, tile), lambda i: (i, 0, 0, 0)),
        ],
        out_specs=block,
        name="update",
    )(state, y_all, w_all, taper)


def solution(mesh):
    in_specs = (P("member", "slab", None, None), P(), P(), P(), P(), P(), P())
    out_specs = P(None, ("slab", "member"))

    return jax.shard_map(on_device, mesh=mesh, in_specs=in_specs, out_specs=out_specs, check_vma=False)
```

```python
import functools
import math

import jax
import jax.numpy as jnp
from jax import lax
from jax.experimental import pallas as pl
from jax.experimental.pallas import tpu as pltpu
from jax.sharding import PartitionSpec as P


COURANT = 0.3
ROTATION = 0.1
HALF = COURANT * 0.5
ROUNDS = 6
TINY = 1e-30
KERNEL_VMEM = 40 * 1024 * 1024
CONVERGED = 1e6
F32 = jnp.float32
BF16 = jnp.bfloat16
VMEM_SPEC = pl.BlockSpec(memory_space=pltpu.VMEM)
SMEM_SPEC = pl.BlockSpec(memory_space=pltpu.SMEM)


def near(*arrays):
    return [pltpu.with_memory_space_constraint(x, pltpu.VMEM) for x in arrays]


def far(*arrays):
    return [pltpu.with_memory_space_constraint(x, pltpu.HBM) for x in arrays]


def kernel_params(limit=KERNEL_VMEM):
    return pltpu.CompilerParams(vmem_limit_bytes=limit)


def d_y(field, scale=1.0):
    width = field.shape[-1]
    axis = field.ndim - 1
    return (pltpu.roll(field, width - 1, axis) - pltpu.roll(field, 1, axis)) * (0.5 * scale)


def split2(x):
    high = x.astype(BF16)
    return high, (x - high.astype(F32)).astype(BF16)


def mm(a, b):
    return lax.dot_general(a, b, (((1,), (0,)), ((), ())), preferred_element_type=F32)


def mm_f32(a, b, dims=((1,), (0,))):
    return lax.dot_general(
        a, b, (dims, ((), ())), precision=lax.Precision.HIGHEST, preferred_element_type=F32
    )


def keep_lanes(ref, start, value):
    rows, width = value.shape
    for c in range(width // 128):
        ref[c, start : start + rows, :] = value[:, c * 128 : (c + 1) * 128]


def every_nth(ref, start, count, stride):
    return jnp.concatenate(
        [ref[c, pl.ds(start, count, stride=stride), :] for c in range(ref.shape[0])], axis=1)


def row_up(field, edge, index):
    rows = field.shape[0]
    return jnp.where(index == rows - 1, edge, pltpu.roll(field, rows - 1, 0))


def row_down(field, edge, index):
    return jnp.where(index == 0, edge, pltpu.roll(field, 1, 0))


def wave_heights(h, u, v):
    rows = h.shape[0]
    index = lax.broadcasted_iota(jnp.int32, h.shape, 0)
    h1 = h - HALF * (row_up(u, 0.0, index) - row_down(u, 0.0, index)) - d_y(v, COURANT)
    below, above = -HALF * u[0:1], HALF * u[rows - 1 : rows]
    u1 = u - HALF * (row_up(h1, above, index) - row_down(h1, below, index)) + ROTATION * v
    v1 = v - d_y(h1, COURANT) - ROTATION * u
    below, above = -HALF * h1[0:1], HALF * h1[rows - 1 : rows]
    h2 = h1 - HALF * (row_up(u1, above, index) - row_down(u1, below, index)) - d_y(v1, COURANT)
    return h2, u1, v1


def edge_rows(h, u, v, sign):
    a = sign * HALF
    dv0 = COURANT * d_y(v[0])
    q = h[0] + a * u[1] - dv0
    h1_1 = h[1] - a * (u[0] - u[2]) - COURANT * d_y(v[1])
    r = u[0] + a * h1_1 + ROTATION * v[0]
    h1_2 = h[2] - a * (u[1] - u[3]) - COURANT * d_y(v[2])
    p = u[1] + a * h1_2 + ROTATION * v[1]
    s = a * p - dv0 + COURANT * ROTATION * d_y(u[0])
    h1 = a * u[0]
    first = (1.0 - 2.0 * HALF * HALF) * h1 + a * r + COURANT * COURANT * d_y(d_y(h1))
    return (u[0], q, r, s), (first, HALF * HALF * q, HALF * HALF * h1)


def prior_kernel(members, cells_x, slabs, batches, me_ref, owner_ref, x_ref, offset_ref,
                 obs_ref, next_ref, prev_ref, mid_ref, rim_ref, rows_ref, lanes_ref):
    cells_y = x_ref.shape[1]
    nobs = offset_ref.shape[1]
    base = members * cells_x
    for m in range(members):
        start = m * 3 * cells_x
        fields = [x_ref[pl.ds(start + f * cells_x, cells_x), :] for f in range(3)]
        after = wave_heights(*fields)
        rows_ref[pl.ds(m * cells_x, cells_x), :] = after[0]
        for f in range(3):
            keep_lanes(lanes_ref, start + f * cells_x, fields[f])
            keep_lanes(mid_ref, start + f * cells_x, after[f])

    def across(field, row):
        return every_nth(lanes_ref, field * cells_x + row, members, 3 * cells_x)

    last = cells_x - 1
    for side, (out_ref, sign) in enumerate(((next_ref, 1.0), (prev_ref, -1.0))):
        rows = [last - i if sign > 0 else i for i in range(4)]
        sent, added = edge_rows(
            [across(0, i) for i in rows[:3]], [across(1, i) for i in rows],
            [across(2, i) for i in rows[:3]], sign)
        for i in range(4):
            out_ref[pl.ds(i * members, members), :] = sent[i]
        for i in range(3):
            rows_ref[pl.ds(base + (3 * side + i) * members, members), :] = added[i]
        rim_ref[pl.ds((1 - side) * members, members), :] = sent[0]

    values = rows_ref[...]
    part0 = values.astype(BF16)
    rest = values - part0.astype(F32)
    part1 = rest.astype(BF16)
    part2 = (rest - part1.astype(F32)).astype(BF16)
    me = me_ref[0]
    total = cells_x * slabs
    for b in range(batches):
        offset = offset_ref[b : b + 1, :]
        column = lax.rem(offset, cells_y)
        row = lax.div(offset, cells_y)
        relative = row + lax.rem(owner_ref[b % slabs] - me + slabs, slabs) * cells_x
        pick = jnp.where(
            lax.broadcasted_iota(jnp.int32, (cells_y, nobs), 0) == column, 1.0, 0.0).astype(BF16)
        found = mm(part0, pick) + (mm(part1, pick) + mm(part2, pick))
        inside = lax.broadcasted_iota(jnp.int32, (cells_x, nobs), 0) == relative
        edges = jnp.zeros((members, nobs), F32)
        for i in range(3):
            piece = found[base + i * members : base + (i + 1) * members]
            edges += jnp.where(relative == cells_x + i, piece, 0.0)
            piece = found[base + (3 + i) * members : base + (4 + i) * members]
            edges += jnp.where(relative == total - 1 - i, piece, 0.0)
        own = [
            jnp.sum(jnp.where(inside, found[m * cells_x : (m + 1) * cells_x], 0.0),
                    axis=0, keepdims=True)
            for m in range(members)
        ]
        whole = jnp.concatenate(own, axis=0) + edges
        at = b * nobs
        place = (pl.ds(at // cells_y * members, members), slice(at % cells_y, at % cells_y + nobs))
        obs_ref[place] = whole


def spot(chunk, cells_y, row, field, column):
    return divmod((row * 3 + field) * cells_y + column, chunk)


def forecast_kernel(members, cells_x, mid_ref, rim_ref, out_ref, rows_ref):
    cells_y = rim_ref.shape[1]
    chunk = out_ref.shape[2]
    piece = math.gcd(chunk, cells_y)
    tiles = range(cells_y // 128)
    index = lax.broadcasted_iota(jnp.int32, (cells_x, cells_y), 0)
    for m in range(members):
        start = m * 3 * cells_x
        h2, u1, v1 = (
            jnp.concatenate([mid_ref[c, start + f * cells_x : start + (f + 1) * cells_x, :] for c in tiles], axis=1)
            for f in range(3))
        u2 = u1 - HALF * (row_up(h2, 0.0, index) - row_down(h2, 0.0, index)) + ROTATION * v1
        v2 = v1 - d_y(h2, COURANT) - ROTATION * u1
        keep_lanes(rows_ref, m * 2 * cells_x, u2)
        keep_lanes(rows_ref, (m * 2 + 1) * cells_x, v2)

    def rim_height(side, sign):
        u = rim_ref[pl.ds(side * members, members), :]
        u1 = every_nth(mid_ref, cells_x + (cells_x - 1) * side, members, 3 * cells_x)
        return sign * HALF * ((1.0 - HALF * HALF) * u + COURANT * COURANT * d_y(d_y(u)) + u1)

    outside = {(0, 1): HALF * rim_height(0, -1.0), (cells_x - 1, 1): -HALF * rim_height(1, 1.0)}
    for r in range(cells_x):
        for f in range(3):
            if f == 0:
                line = every_nth(mid_ref, r, members, 3 * cells_x)
            else:
                line = every_nth(rows_ref, (f - 1) * cells_x + r, members, 2 * cells_x)
            if (r, f) in outside:
                line = line + outside[r, f]
            for c in range(0, cells_y, piece):
                dest, lane = spot(chunk, cells_y, r, f, c)
                out_ref[dest, :, lane : lane + piece] = line[:, c : c + piece]


def edge_forecast(message, members, sign):
    a = sign * HALF
    u, q, r, s = (message[i * members : (i + 1) * members] for i in range(4))
    square = COURANT * COURANT
    h1 = a * u
    u1_0, u1_1 = a * q, a * h1
    v1 = -d_y(h1, COURANT)
    h2_0 = (1.0 - 2.0 * a * a) * h1 + a * r + square * d_y(d_y(h1))
    h2_1, h2_2 = a * u1_0, a * u1_1
    h2_edge = (1.0 - 2.0 * a * a) * q + square * d_y(d_y(q)) + s
    return {
        (0, 0): h2_0, (1, 0): h2_1, (2, 0): h2_2,
        (0, 1): u1_0 - a * (h2_1 - h2_edge) + ROTATION * v1,
        (1, 1): u1_1 - a * (h2_2 - h2_0), (2, 1): a * h2_1, (3, 1): a * h2_2,
        (0, 2): v1 - COURANT * d_y(h2_0) - ROTATION * u1_0,
        (1, 2): -COURANT * d_y(h2_1) - ROTATION * u1_1, (2, 2): -COURANT * d_y(h2_2),
    }


def correct_kernel(members, cells_x, low_ref, high_ref, in_ref, out_ref):
    cells_y = low_ref.shape[1]
    chunk = out_ref.shape[2]
    piece = math.gcd(chunk, cells_y)
    out_ref[...] = in_ref[...]
    for ref, sign in ((low_ref, 1.0), (high_ref, -1.0)):
        for (i, f), value in edge_forecast(ref[...], members, sign).items():
            row = i if sign > 0 else cells_x - 1 - i
            for c in range(0, cells_y, piece):
                dest, lane = spot(chunk, cells_y, row, f, c)
                at = (dest, slice(None), slice(lane, lane + piece))
                out_ref[at] = in_ref[at] + value[:, c : c + piece]


def stack_kernel(*refs):
    rows = refs[0].shape[0]
    for k, ref in enumerate(refs[:-1]):
        refs[-1][k * rows : (k + 1) * rows, :] = ref[...]


def sum_kernel(*refs):
    total = refs[0][...]
    for ref in refs[1:-1]:
        total = total + ref[...]
    refs[-1][...] = total


def column_of(row, lanes=128):
    return jnp.transpose(jnp.broadcast_to(row, (lanes,) + row.shape[1:]))


def gap2(a, b, around, inverse):
    gap = jnp.abs(a - b)
    gap = jnp.minimum(gap, around - gap) * inverse
    return gap * gap


def taper_of(squared):
    ramp = jnp.maximum(0.0, 1.0 - squared * lax.rsqrt(squared))
    return ramp * ramp


def geometry(owner_ref, offset_ref, cutoff_ref, b, slabs, cells_x, cells_y):
    offset = offset_ref[b : b + 1, :]
    row = lax.div(offset, cells_y) + owner_ref[b % slabs] * cells_x
    column = lax.rem(offset, cells_y)
    return row.astype(F32), column.astype(F32), 1.0 / cutoff_ref[b : b + 1, :].astype(F32)


def taper_kernel(slabs, cells_x, cells_y, batches, tile, groups, first_ref, owner_ref, offset_ref,
                 cutoff_ref, out_ref):
    starts = [first_ref[0] + at for at in groups]
    columns = {}
    for g, at in enumerate(groups):
        columns.setdefault(at % cells_y, []).append(g)
    for b in range(batches):
        row, column, inverse = (
            column_of(x) for x in geometry(owner_ref, offset_ref, cutoff_ref, b, slabs, cells_x, cells_y))
        rows = [gap2(lax.div(start, 3 * cells_y).astype(F32), row, float(cells_x * slabs), inverse)
                for start in starts]
        for members in columns.values():
            for lane in range(0, tile, 128):
                cell = (lax.rem(starts[members[0]], cells_y) + lane
                        + lax.broadcasted_iota(jnp.int32, (1, 128), 1)).astype(F32)
                gap_y = jnp.maximum(gap2(cell, column, float(cells_y), inverse), TINY)
                for g in members:
                    out_ref[g, b, :, lane : lane + 128] = taper_of(gap_y + rows[g])


def solve_members(gram, right, lowest, work_ref):
    size = gram.shape[0]
    top = jnp.max(jnp.sum(jnp.abs(gram), axis=1, keepdims=True), axis=0, keepdims=True)
    top = jnp.maximum(top, 4.0 * lowest)
    eye = jnp.where(
        lax.broadcasted_iota(jnp.int32, (size, size), 0)
        == lax.broadcasted_iota(jnp.int32, (size, size), 1), 1.0, 0.0)
    alpha = 2.0 / (top + lowest)

    def double(r, x, t):
        t = 2.0 * t * t - 1.0
        extra = 1.0 / t
        both = mm_f32(r, jnp.concatenate([r, x], axis=1))
        gain = 1.0 + extra
        return gain * both[:, :size] - extra * eye, gain * (x + both[:, size:]), t

    r, x, t = eye - alpha * gram, alpha * right, (top + lowest) / (top - lowest)
    for _ in range(ROUNDS):
        r, x, t = double(r, x, t)
    work_ref[:, :size] = r
    work_ref[:, size:] = x

    def more(t):
        r, x, t = double(work_ref[:, :size], work_ref[:, size:], jnp.full((1, 1), t, F32))
        work_ref[:, :size] = r
        work_ref[:, size:] = x
        return t[0, 0]

    lax.while_loop(lambda t: t < CONVERGED, more, t[0, 0])
    return work_ref[:, size:]


def stack3(state):
    high, low = split2(state - jnp.mean(state, axis=0, keepdims=True))
    return jnp.concatenate([high, low, high], axis=0)


def weigh(pair, high, low):
    members = pair.shape[0] // 2
    main, rest = mm(pair, high), mm(pair, low)
    return main[:members] + (main[members:] + rest[:members])


def chain_kernel(slabs, cells_x, cells_y, batches, parts, *refs):
    member_ref, owner_ref, offset_ref, cutoff_ref, values_ref, variance_ref, perturb_ref = refs[:7]
    y_ref, w_ref, obs_ref, work_ref = refs[9:]
    members = obs_ref.shape[0]
    nobs = offset_ref.shape[1]
    each = members // parts
    scale = 1.0 / (members - 1)
    blocks = obs_ref.shape[1] // cells_y
    for k in range(parts):
        half, by = divmod(k, parts // 2)
        source = lax.rem((member_ref[0] ^ half) - 2 * by + parts, parts)
        at = pl.ds(pl.multiple_of(source * each, each), each)
        for c in range(blocks):
            first = (by * blocks + c) * each
            obs_ref[at, c * cells_y : (c + 1) * cells_y] = refs[7 + half][first : first + each, :]
    eye = (lax.broadcasted_iota(jnp.int32, (members, members), 0)
           == lax.broadcasted_iota(jnp.int32, (members, members), 1))
    places = [geometry(owner_ref, offset_ref, cutoff_ref, b, slabs, cells_x, cells_y)
              for b in range(batches)]
    for b in range(batches):
        observed = obs_ref[:, b * nobs : (b + 1) * nobs]
        spread = observed - jnp.mean(observed, axis=0, keepdims=True)
        variance = variance_ref[b : b + 1, :]
        inverse = 1.0 / variance
        target = values_ref[b : b + 1, :] + jnp.sqrt(variance) * perturb_ref[b] - observed
        both = mm_f32(spread * inverse, jnp.concatenate([spread, target], axis=0), ((1,), (1,)))
        gram = both[:, :members] + jnp.where(eye, float(members - 1), 0.0)
        high, low = split2(jnp.transpose(spread) * scale)
        spread_t = jnp.concatenate([high, high, low], axis=1)
        y_ref[b] = spread_t
        if b + 1 < batches:
            later = obs_ref[:, (b + 1) * nobs :]
            row, column, inverse_cutoff = (column_of(x) for x in places[b])
            tapers = []
            for c in range(b + 1, batches):
                for lane in range(0, nobs, 128):
                    row_j, column_j = (x[:, lane : lane + 128] for x in places[c][:2])
                    squared = (gap2(row_j, row, float(cells_x * slabs), inverse_cutoff)
                               + gap2(column_j, column, float(cells_y), inverse_cutoff))
                    tapers.append(taper_of(jnp.maximum(squared, TINY)))
            gain_high, gain_low = split2(
                mm(spread_t, stack3(later)) * jnp.concatenate(tapers, axis=1))
        solved = solve_members(gram, both[:, members:], float(members - 1), work_ref)
        weights = (target - mm_f32(solved, spread, ((0,), (0,)))) * inverse
        high, low = split2(weights)
        pair = jnp.concatenate([high, low], axis=0)
        w_ref[b] = pair
        if b + 1 < batches:
            obs_ref[:, (b + 1) * nobs :] = later + weigh(pair, gain_high, gain_low)


def update_kernel(batches, tile, groups, s_ref, y_ref, w_ref, taper_ref, out_ref):
    step = pl.program_id(0)
    width = out_ref.shape[1]
    for b in range(batches):
        for g, tiles in enumerate(groups):
            for at in tiles:
                if b:
                    state = out_ref[:, at : at + tile]
                else:
                    state = s_ref[:, pl.ds(pl.multiple_of(step * width + at, 128), tile)]
                covariance = mm(y_ref[b], stack3(state))
                high, low = split2(covariance * taper_ref[g, b])
                out_ref[:, at : at + tile] = state + weigh(w_ref[b], high, low)


def on_device(prior, obs_values, obs_variance, obs_perturb, obs_offset, owner_order, taper_cutoff):
    slabs = lax.axis_size("slab")
    shards = lax.axis_size("member")
    each, cells_x, _, cells_y = prior.shape
    batches, nobs = obs_values.shape
    members = each * shards
    chunk = 3 * cells_x * cells_y // shards
    slab = lax.axis_index("slab")
    member = lax.axis_index("member")
    x = prior.transpose(0, 2, 1, 3).reshape(each * 3 * cells_x, cells_y)
    owner = owner_order.astype(jnp.int32)
    perturb = obs_perturb.transpose(0, 2, 1)

    def shift(count, by):
        return [(i, (i + by) % count) for i in range(count)]

    lines = batches * nobs // cells_y * each
    message = pltpu.VMEM((4 * each, cells_y), F32)
    lane_tiles = (cells_y // 128, each * 3 * cells_x, 128)
    partial, to_next, to_prev, mid, rim = pl.pallas_call(
        functools.partial(prior_kernel, each, cells_x, slabs, batches),
        out_shape=(
            pltpu.VMEM((lines, cells_y), F32), message, message,
            pltpu.VMEM(lane_tiles, F32), pltpu.VMEM((2 * each, cells_y), F32),
        ),
        in_specs=[SMEM_SPEC, SMEM_SPEC, VMEM_SPEC, VMEM_SPEC],
        out_specs=(VMEM_SPEC,) * 5,
        scratch_shapes=[
            pltpu.VMEM((each * cells_x + 6 * each, cells_y), F32),
            pltpu.VMEM(lane_tiles, F32),
        ],
        compiler_params=kernel_params(),
        name="prior",
    )(slab.reshape(1), *far(owner, x, obs_offset))
    low = lax.ppermute(to_next, "slab", shift(slabs, 1))
    high = lax.ppermute(to_prev, "slab", shift(slabs, -1))
    pieces = [partial] + [
        lax.ppermute(partial, "member", shift(shards, by)) for by in range(2, shards, 2)]

    outgoing = pltpu.VMEM((shards, each, chunk), F32)
    inner = pl.pallas_call(
        functools.partial(forecast_kernel, each, cells_x),
        out_shape=outgoing,
        in_specs=[VMEM_SPEC] * 2,
        out_specs=VMEM_SPEC,
        scratch_shapes=[pltpu.VMEM((cells_y // 128, each * 2 * cells_x, 128), F32)],
        compiler_params=kernel_params(),
        name="forecast",
    )(*near(mid, rim))
    outgoing = pl.pallas_call(
        functools.partial(correct_kernel, each, cells_x),
        out_shape=outgoing,
        in_specs=[VMEM_SPEC] * 3,
        out_specs=VMEM_SPEC,
        compiler_params=kernel_params(),
        name="correct",
    )(*near(low, high, inner))

    state = lax.all_to_all(outgoing, "member", 0, 0).reshape(members, chunk)

    gathered = pltpu.VMEM((len(pieces) * lines, cells_y), F32)
    stacked = pl.pallas_call(
        stack_kernel, out_shape=gathered, in_specs=[VMEM_SPEC] * len(pieces), out_specs=VMEM_SPEC,
        compiler_params=kernel_params(), name="stack",
    )(*near(*pieces))
    parts = [stacked] + [lax.ppermute(stacked, "slab", shift(slabs, by)) for by in range(1, slabs)]
    observed = pl.pallas_call(
        sum_kernel, out_shape=gathered, in_specs=[VMEM_SPEC] * slabs, out_specs=VMEM_SPEC,
        compiler_params=kernel_params(), name="sum",
    )(*near(*parts))
    partner = lax.ppermute(observed, "member", [(i, i ^ 1) for i in range(shards)])

    steps = max(1, chunk // (3 * cells_y))
    width = chunk // steps
    tile = math.gcd(width, 256)
    if width == 3 * cells_y:
        groups = [[f * cells_y + c for f in range(3)] for c in range(0, cells_y, tile)]
    else:
        groups = [[at] for at in range(0, width, tile)]
    firsts = [i * width + g[0] for i in range(steps) for g in groups]
    first = (slab * shards + member) * chunk
    taper = pl.pallas_call(
        functools.partial(
            taper_kernel, slabs, cells_x, cells_y, batches, tile, firsts),
        out_shape=pltpu.HBM((len(firsts), batches, nobs, tile), F32),
        in_specs=[SMEM_SPEC, SMEM_SPEC, VMEM_SPEC, VMEM_SPEC],
        out_specs=VMEM_SPEC,
        compiler_params=kernel_params(),
        name="taper",
    )(first.reshape(1), owner, obs_offset, taper_cutoff)

    chain = pl.pallas_call(
        functools.partial(chain_kernel, slabs, cells_x, cells_y, batches, shards),
        out_shape=(
            pltpu.VMEM((batches, nobs, 3 * members), BF16),
            pltpu.VMEM((batches, 2 * members, nobs), BF16),
        ),
        in_specs=[SMEM_SPEC, SMEM_SPEC] + [VMEM_SPEC] * 7,
        out_specs=(VMEM_SPEC,) * 2,
        scratch_shapes=[
            pltpu.VMEM((members, batches * nobs), F32),
            pltpu.VMEM((members, 2 * members), F32),
        ],
        compiler_params=kernel_params(),
        name="chain",
    )
    y_all, w_all = chain(
        member.reshape(1), owner, obs_offset, taper_cutoff, obs_values, obs_variance, perturb, *near(observed, partner))

    block = pl.BlockSpec((members, width), lambda i: (0, i))
    return pl.pallas_call(
        functools.partial(update_kernel, batches, tile, groups),
        grid=(steps,),
        out_shape=jax.ShapeDtypeStruct((members, chunk), F32),
        in_specs=[VMEM_SPEC] * 3 + [pl.BlockSpec((len(groups), batches, nobs, tile), lambda i: (i, 0, 0, 0))],
        out_specs=block,
        compiler_params=kernel_params(),
        name="update",
    )(*near(state, y_all, w_all), *far(taper))


def solution(mesh):
    in_specs = (P("member", "slab", None, None), P(), P(), P(), P(), P(), P())
    out_specs = P(None, ("slab", "member"))

    return jax.shard_map(on_device, mesh=mesh, in_specs=in_specs, out_specs=out_specs, check_vma=False)
```

```python
import functools
import math

import jax
import jax.numpy as jnp
from jax import lax
from jax.experimental import pallas as pl
from jax.experimental.pallas import tpu as pltpu
from jax.sharding import PartitionSpec as P


COURANT = 0.3
ROTATION = 0.1
HALF = COURANT * 0.5
ROUNDS = 6
KEPT = 2
TINY = 1e-30
KERNEL_VMEM = 40 * 1024 * 1024
CONVERGED = 1e6
LEAST = 1.0 + 1e-6
F32 = jnp.float32
BF16 = jnp.bfloat16
VMEM_SPEC = pl.BlockSpec(memory_space=pltpu.VMEM)
ANY_SPEC = pl.BlockSpec(memory_space=pl.ANY)
SMEM_SPEC = pl.BlockSpec(memory_space=pltpu.SMEM)


def near(*arrays):
    return [pltpu.with_memory_space_constraint(x, pltpu.VMEM) for x in arrays]


def far(*arrays):
    return [pltpu.with_memory_space_constraint(x, pltpu.HBM) for x in arrays]


def kernel_params(limit=KERNEL_VMEM):
    return pltpu.CompilerParams(vmem_limit_bytes=limit)


def d_y(field, scale=1.0):
    width = field.shape[-1]
    axis = field.ndim - 1
    return (pltpu.roll(field, width - 1, axis) - pltpu.roll(field, 1, axis)) * (0.5 * scale)


def split2(x):
    high = x.astype(BF16)
    return high, (x - high.astype(F32)).astype(BF16)


def mm(a, b):
    return lax.dot_general(a, b, (((1,), (0,)), ((), ())), preferred_element_type=F32)


def mm_f32(a, b, dims=((1,), (0,))):
    return lax.dot_general(
        a, b, (dims, ((), ())), precision=lax.Precision.HIGHEST, preferred_element_type=F32
    )


def keep_lanes(ref, start, value):
    rows, width = value.shape
    for c in range(width // 128):
        ref[c, start : start + rows, :] = value[:, c * 128 : (c + 1) * 128]


def every_nth(ref, start, count, stride):
    return jnp.concatenate(
        [ref[c, pl.ds(start, count, stride=stride), :] for c in range(ref.shape[0])], axis=1)


def row_up(field, edge, index):
    rows = field.shape[0]
    return jnp.where(index == rows - 1, edge, pltpu.roll(field, rows - 1, 0))


def row_down(field, edge, index):
    return jnp.where(index == 0, edge, pltpu.roll(field, 1, 0))


def wave_heights(h, u, v):
    rows = h.shape[0]
    index = lax.broadcasted_iota(jnp.int32, h.shape, 0)
    h1 = h - HALF * (row_up(u, 0.0, index) - row_down(u, 0.0, index)) - d_y(v, COURANT)
    below, above = -HALF * u[0:1], HALF * u[rows - 1 : rows]
    u1 = u - HALF * (row_up(h1, above, index) - row_down(h1, below, index)) + ROTATION * v
    v1 = v - d_y(h1, COURANT) - ROTATION * u
    below, above = -HALF * h1[0:1], HALF * h1[rows - 1 : rows]
    h2 = h1 - HALF * (row_up(u1, above, index) - row_down(u1, below, index)) - d_y(v1, COURANT)
    return h2, u1, v1


def edge_rows(h, u, v, sign):
    a = sign * HALF
    dv0 = COURANT * d_y(v[0])
    q = h[0] + a * u[1] - dv0
    h1_1 = h[1] - a * (u[0] - u[2]) - COURANT * d_y(v[1])
    r = u[0] + a * h1_1 + ROTATION * v[0]
    h1_2 = h[2] - a * (u[1] - u[3]) - COURANT * d_y(v[2])
    p = u[1] + a * h1_2 + ROTATION * v[1]
    s = a * p - dv0 + COURANT * ROTATION * d_y(u[0])
    h1 = a * u[0]
    first = (1.0 - 2.0 * HALF * HALF) * h1 + a * r + COURANT * COURANT * d_y(d_y(h1))
    return (u[0], q, r, s), (first, HALF * HALF * q, HALF * HALF * h1)


def prior_kernel(members, cells_x, slabs, batches, me_ref, owner_ref, x_ref, offset_ref,
                 obs_ref, next_ref, prev_ref, mid_ref, rim_ref, rows_ref, lanes_ref):
    cells_y = x_ref.shape[1]
    nobs = offset_ref.shape[1]
    base = members * cells_x
    for m in range(members):
        start = m * 3 * cells_x
        fields = [x_ref[pl.ds(start + f * cells_x, cells_x), :] for f in range(3)]
        after = wave_heights(*fields)
        rows_ref[pl.ds(m * cells_x, cells_x), :] = after[0]
        for f in range(3):
            keep_lanes(lanes_ref, start + f * cells_x, fields[f])
            keep_lanes(mid_ref, start + f * cells_x, after[f])

    def across(field, row):
        return every_nth(lanes_ref, field * cells_x + row, members, 3 * cells_x)

    last = cells_x - 1
    for side, (out_ref, sign) in enumerate(((next_ref, 1.0), (prev_ref, -1.0))):
        rows = [last - i if sign > 0 else i for i in range(4)]
        sent, added = edge_rows(
            [across(0, i) for i in rows[:3]], [across(1, i) for i in rows],
            [across(2, i) for i in rows[:3]], sign)
        for i in range(4):
            out_ref[pl.ds(i * members, members), :] = sent[i]
        for i in range(3):
            rows_ref[pl.ds(base + (3 * side + i) * members, members), :] = added[i]
        rim_ref[pl.ds((1 - side) * members, members), :] = sent[0]

    values = rows_ref[...]
    part0 = values.astype(BF16)
    rest = values - part0.astype(F32)
    part1 = rest.astype(BF16)
    part2 = (rest - part1.astype(F32)).astype(BF16)
    me = me_ref[0]
    total = cells_x * slabs
    for b in range(batches):
        offset = offset_ref[b : b + 1, :]
        column = lax.rem(offset, cells_y)
        row = lax.div(offset, cells_y)
        relative = row + lax.rem(owner_ref[b % slabs] - me + slabs, slabs) * cells_x
        pick = jnp.where(
            lax.broadcasted_iota(jnp.int32, (cells_y, nobs), 0) == column, 1.0, 0.0).astype(BF16)
        found = mm(part0, pick) + (mm(part1, pick) + mm(part2, pick))
        inside = lax.broadcasted_iota(jnp.int32, (cells_x, nobs), 0) == relative
        edges = jnp.zeros((members, nobs), F32)
        for i in range(3):
            piece = found[base + i * members : base + (i + 1) * members]
            edges += jnp.where(relative == cells_x + i, piece, 0.0)
            piece = found[base + (3 + i) * members : base + (4 + i) * members]
            edges += jnp.where(relative == total - 1 - i, piece, 0.0)
        own = [
            jnp.sum(jnp.where(inside, found[m * cells_x : (m + 1) * cells_x], 0.0),
                    axis=0, keepdims=True)
            for m in range(members)
        ]
        whole = jnp.concatenate(own, axis=0) + edges
        at = b * nobs
        place = (pl.ds(at // cells_y * members, members), slice(at % cells_y, at % cells_y + nobs))
        obs_ref[place] = whole


def spot(chunk, cells_y, row, field, column):
    return divmod((row * 3 + field) * cells_y + column, chunk)


def forecast_kernel(members, cells_x, mid_ref, rim_ref, out_ref, rows_ref):
    cells_y = rim_ref.shape[1]
    chunk = out_ref.shape[2]
    piece = math.gcd(chunk, cells_y)
    tiles = range(cells_y // 128)
    index = lax.broadcasted_iota(jnp.int32, (cells_x, cells_y), 0)
    for m in range(members):
        start = m * 3 * cells_x
        h2, u1, v1 = (
            jnp.concatenate([mid_ref[c, start + f * cells_x : start + (f + 1) * cells_x, :] for c in tiles], axis=1)
            for f in range(3))
        u2 = u1 - HALF * (row_up(h2, 0.0, index) - row_down(h2, 0.0, index)) + ROTATION * v1
        v2 = v1 - d_y(h2, COURANT) - ROTATION * u1
        keep_lanes(rows_ref, m * 2 * cells_x, u2)
        keep_lanes(rows_ref, (m * 2 + 1) * cells_x, v2)

    def rim_height(side, sign):
        u = rim_ref[pl.ds(side * members, members), :]
        u1 = every_nth(mid_ref, cells_x + (cells_x - 1) * side, members, 3 * cells_x)
        return sign * HALF * ((1.0 - HALF * HALF) * u + COURANT * COURANT * d_y(d_y(u)) + u1)

    outside = {(0, 1): HALF * rim_height(0, -1.0), (cells_x - 1, 1): -HALF * rim_height(1, 1.0)}
    for r in range(cells_x):
        for f in range(3):
            if f == 0:
                line = every_nth(mid_ref, r, members, 3 * cells_x)
            else:
                line = every_nth(rows_ref, (f - 1) * cells_x + r, members, 2 * cells_x)
            if (r, f) in outside:
                line = line + outside[r, f]
            for c in range(0, cells_y, piece):
                dest, lane = spot(chunk, cells_y, r, f, c)
                out_ref[dest, :, lane : lane + piece] = line[:, c : c + piece]


def edge_forecast(message, members, sign):
    a = sign * HALF
    u, q, r, s = (message[i * members : (i + 1) * members] for i in range(4))
    square = COURANT * COURANT
    h1 = a * u
    u1_0, u1_1 = a * q, a * h1
    v1 = -d_y(h1, COURANT)
    h2_0 = (1.0 - 2.0 * a * a) * h1 + a * r + square * d_y(d_y(h1))
    h2_1, h2_2 = a * u1_0, a * u1_1
    h2_edge = (1.0 - 2.0 * a * a) * q + square * d_y(d_y(q)) + s
    return {
        (0, 0): h2_0, (1, 0): h2_1, (2, 0): h2_2,
        (0, 1): u1_0 - a * (h2_1 - h2_edge) + ROTATION * v1,
        (1, 1): u1_1 - a * (h2_2 - h2_0), (2, 1): a * h2_1, (3, 1): a * h2_2,
        (0, 2): v1 - COURANT * d_y(h2_0) - ROTATION * u1_0,
        (1, 2): -COURANT * d_y(h2_1) - ROTATION * u1_1, (2, 2): -COURANT * d_y(h2_2),
    }


def correct_kernel(members, cells_x, low_ref, high_ref, in_ref, out_ref):
    cells_y = low_ref.shape[1]
    chunk = out_ref.shape[2]
    piece = math.gcd(chunk, cells_y)
    out_ref[...] = in_ref[...]
    for ref, sign in ((low_ref, 1.0), (high_ref, -1.0)):
        for (i, f), value in edge_forecast(ref[...], members, sign).items():
            row = i if sign > 0 else cells_x - 1 - i
            for c in range(0, cells_y, piece):
                dest, lane = spot(chunk, cells_y, row, f, c)
                at = (dest, slice(None), slice(lane, lane + piece))
                out_ref[at] = in_ref[at] + value[:, c : c + piece]


def stack_kernel(*refs):
    rows = refs[0].shape[0]
    for k, ref in enumerate(refs[:-1]):
        refs[-1][k * rows : (k + 1) * rows, :] = ref[...]


def sum_kernel(*refs):
    total = refs[0][...]
    for ref in refs[1:-1]:
        total = total + ref[...]
    refs[-1][...] = total


def column_of(row, lanes=128):
    return jnp.transpose(jnp.broadcast_to(row, (lanes,) + row.shape[1:]))


def gap2(a, b, around, inverse):
    gap = jnp.abs(a - b)
    gap = jnp.minimum(gap, around - gap) * inverse
    return gap * gap


def taper_of(squared):
    ramp = jnp.maximum(0.0, 1.0 - squared * lax.rsqrt(squared))
    return ramp * ramp


def geometry(owner_ref, offset_ref, cutoff_ref, b, slabs, cells_x, cells_y):
    offset = offset_ref[b : b + 1, :]
    row = lax.div(offset, cells_y) + owner_ref[b % slabs] * cells_x
    column = lax.rem(offset, cells_y)
    return row.astype(F32), column.astype(F32), 1.0 / cutoff_ref[b : b + 1, :].astype(F32)


def taper_kernel(slabs, cells_x, cells_y, batches, tile, count, groups, first_ref, owner_ref, offset_ref,
                 cutoff_ref, near_ref, far_ref):
    kept = near_ref.shape[0]
    starts = [first_ref[0] + at for at in groups]
    columns = {}
    for g, at in enumerate(groups):
        columns.setdefault(at % cells_y, []).append(g)
    for b in range(batches):
        row, column, inverse = (
            column_of(x) for x in geometry(owner_ref, offset_ref, cutoff_ref, b, slabs, cells_x, cells_y))
        rows = [gap2(lax.div(start, 3 * cells_y).astype(F32), row, float(cells_x * slabs), inverse)
                for start in starts]
        for members in columns.values():
            for lane in range(0, tile, 128):
                cell = (lax.rem(starts[members[0]], cells_y) + lane
                        + lax.broadcasted_iota(jnp.int32, (1, 128), 1)).astype(F32)
                gap_y = jnp.maximum(gap2(cell, column, float(cells_y), inverse), TINY)
                for g in members:
                    at = (g // count * batches + b) * count + g % count
                    ref, at = (near_ref, at) if at < kept else (far_ref, at - kept)
                    ref[at, :, lane : lane + 128] = taper_of(gap_y + rows[g])


def solve_members(gram, right, lowest, work_ref):
    size = gram.shape[0]
    top = jnp.max(jnp.sum(jnp.abs(gram), axis=1, keepdims=True), axis=0, keepdims=True)
    top = jnp.maximum(top, 4.0 * lowest)
    eye = jnp.where(
        lax.broadcasted_iota(jnp.int32, (size, size), 0)
        == lax.broadcasted_iota(jnp.int32, (size, size), 1), 1.0, 0.0)
    alpha = 2.0 / (top + lowest)

    def double(r, x, t):
        t = 2.0 * t * t - 1.0
        extra = 1.0 / t
        both = mm_f32(r, jnp.concatenate([r, x], axis=1))
        gain = 1.0 + extra
        return gain * both[:, :size] - extra * eye, gain * (x + both[:, size:]), t

    t = jnp.maximum((top + lowest) / (top - lowest), LEAST)
    r, x = eye - alpha * gram, alpha * right
    for _ in range(ROUNDS):
        r, x, t = double(r, x, t)
    work_ref[:, :size] = r
    work_ref[:, size:] = x

    def more(t):
        r, x, t = double(work_ref[:, :size], work_ref[:, size:], jnp.full((1, 1), t, F32))
        work_ref[:, :size] = r
        work_ref[:, size:] = x
        return t[0, 0]

    lax.while_loop(lambda t: t < CONVERGED, more, t[0, 0])
    return work_ref[:, size:]


def stack3(state):
    high, low = split2(state - jnp.mean(state, axis=0, keepdims=True))
    return jnp.concatenate([high, low, high], axis=0)


def weigh(pair, high, low):
    members = pair.shape[0] // 2
    main, rest = mm(pair, high), mm(pair, low)
    return main[:members] + (main[members:] + rest[:members])


def chain_kernel(slabs, cells_x, cells_y, batches, parts, *refs):
    member_ref, owner_ref, offset_ref, cutoff_ref, values_ref, variance_ref, perturb_ref = refs[:7]
    y_ref, w_ref, obs_ref, work_ref = refs[9:]
    members = obs_ref.shape[0]
    nobs = offset_ref.shape[1]
    each = members // parts
    scale = 1.0 / (members - 1)
    blocks = obs_ref.shape[1] // cells_y
    for k in range(parts):
        half, by = divmod(k, parts // 2)
        source = lax.rem((member_ref[0] ^ half) - 2 * by + parts, parts)
        at = pl.ds(pl.multiple_of(source * each, each), each)
        for c in range(blocks):
            first = (by * blocks + c) * each
            obs_ref[at, c * cells_y : (c + 1) * cells_y] = refs[7 + half][first : first + each, :]
    eye = (lax.broadcasted_iota(jnp.int32, (members, members), 0)
           == lax.broadcasted_iota(jnp.int32, (members, members), 1))
    places = [geometry(owner_ref, offset_ref, cutoff_ref, b, slabs, cells_x, cells_y)
              for b in range(batches)]
    for b in range(batches):
        observed = obs_ref[:, b * nobs : (b + 1) * nobs]
        spread = observed - jnp.mean(observed, axis=0, keepdims=True)
        variance = variance_ref[b : b + 1, :]
        inverse = 1.0 / variance
        target = values_ref[b : b + 1, :] + jnp.sqrt(variance) * perturb_ref[b] - observed
        both = mm_f32(spread * inverse, jnp.concatenate([spread, target], axis=0), ((1,), (1,)))
        gram = both[:, :members] + jnp.where(eye, float(members - 1), 0.0)
        high, low = split2(jnp.transpose(spread) * scale)
        spread_t = jnp.concatenate([high, high, low], axis=1)
        y_ref[b] = spread_t
        if b + 1 < batches:
            later = obs_ref[:, (b + 1) * nobs :]
            row, column, inverse_cutoff = (column_of(x) for x in places[b])
            tapers = []
            for c in range(b + 1, batches):
                for lane in range(0, nobs, 128):
                    row_j, column_j = (x[:, lane : lane + 128] for x in places[c][:2])
                    squared = (gap2(row_j, row, float(cells_x * slabs), inverse_cutoff)
                               + gap2(column_j, column, float(cells_y), inverse_cutoff))
                    tapers.append(taper_of(jnp.maximum(squared, TINY)))
            gain_high, gain_low = split2(
                mm(spread_t, stack3(later)) * jnp.concatenate(tapers, axis=1))
        solved = solve_members(gram, both[:, members:], float(members - 1), work_ref)
        weights = (target - mm_f32(solved, spread, ((0,), (0,)))) * inverse
        high, low = split2(weights)
        pair = jnp.concatenate([high, low], axis=0)
        w_ref[b] = pair
        if b + 1 < batches:
            obs_ref[:, (b + 1) * nobs :] = later + weigh(pair, gain_high, gain_low)


def update_kernel(batches, tile, groups, width, s_ref, y_ref, w_ref, near_ref, far_ref,
                  out_ref, result_ref, copy_ref, sems):
    steps = s_ref.shape[1] // width
    count = len(groups)
    kept = near_ref.shape[0]
    bounds = [0] + [(step + 1) * batches * count - kept for step in range(steps)]
    fetches = [
        pltpu.make_async_copy(far_ref.at[pl.ds(a, b - a)], copy_ref.at[pl.ds(a, b - a)], sems.at[i])
        for i, (a, b) in enumerate(zip(bounds, bounds[1:]))]
    for fetch in fetches:
        fetch.start()
    sent = []
    for step in range(steps):
        for b in range(batches):
            entry = (step * batches + b) * count - kept
            if entry in bounds:
                fetches[step].wait()
            for g, tiles in enumerate(groups):
                for at in tiles:
                    at = step * width + at
                    state = (result_ref if b else s_ref)[:, at : at + tile]
                    covariance = mm(y_ref[b], stack3(state))
                    taper = copy_ref[entry + g] if entry >= 0 else near_ref[entry + g + kept]
                    high, low = split2(covariance * taper)
                    pair = w_ref[b]
                    half = pair.shape[0] // 2
                    two, one = mm(pair, high), mm(pair[:half], low)
                    result_ref[:, at : at + tile] = state + (two[:half] + (two[half:] + one))
        span = pl.ds(step * width, width)
        sent.append(pltpu.make_async_copy(
            result_ref.at[:, span], out_ref.at[:, span], sems.at[steps + step]))
        sent[-1].start()
    for copy in sent:
        copy.wait()


def on_device(prior, obs_values, obs_variance, obs_perturb, obs_offset, owner_order, taper_cutoff):
    slabs = lax.axis_size("slab")
    shards = lax.axis_size("member")
    each, cells_x, _, cells_y = prior.shape
    batches, nobs = obs_values.shape
    members = each * shards
    chunk = 3 * cells_x * cells_y // shards
    slab = lax.axis_index("slab")
    member = lax.axis_index("member")
    x = prior.transpose(0, 2, 1, 3).reshape(each * 3 * cells_x, cells_y)
    owner = owner_order.astype(jnp.int32)
    perturb = obs_perturb.transpose(0, 2, 1)

    def shift(count, by):
        return [(i, (i + by) % count) for i in range(count)]

    lines = batches * nobs // cells_y * each
    message = pltpu.VMEM((4 * each, cells_y), F32)
    lane_tiles = (cells_y // 128, each * 3 * cells_x, 128)
    partial, to_next, to_prev, mid, rim = pl.pallas_call(
        functools.partial(prior_kernel, each, cells_x, slabs, batches),
        out_shape=(
            pltpu.VMEM((lines, cells_y), F32), message, message,
            pltpu.VMEM(lane_tiles, F32), pltpu.VMEM((2 * each, cells_y), F32),
        ),
        in_specs=[SMEM_SPEC, SMEM_SPEC, VMEM_SPEC, VMEM_SPEC],
        out_specs=(VMEM_SPEC,) * 5,
        scratch_shapes=[
            pltpu.VMEM((each * cells_x + 6 * each, cells_y), F32),
            pltpu.VMEM(lane_tiles, F32),
        ],
        compiler_params=kernel_params(),
        name="prior",
    )(slab.reshape(1), *far(owner, x, obs_offset))
    low = lax.ppermute(to_next, "slab", shift(slabs, 1))
    high = lax.ppermute(to_prev, "slab", shift(slabs, -1))
    pieces = [partial] + [
        lax.ppermute(partial, "member", shift(shards, by)) for by in range(2, shards, 2)]

    outgoing = pltpu.VMEM((shards, each, chunk), F32)
    inner = pl.pallas_call(
        functools.partial(forecast_kernel, each, cells_x),
        out_shape=outgoing,
        in_specs=[VMEM_SPEC] * 2,
        out_specs=VMEM_SPEC,
        scratch_shapes=[pltpu.VMEM((cells_y // 128, each * 2 * cells_x, 128), F32)],
        compiler_params=kernel_params(),
        name="forecast",
    )(*near(mid, rim))
    outgoing = pl.pallas_call(
        functools.partial(correct_kernel, each, cells_x),
        out_shape=outgoing,
        in_specs=[VMEM_SPEC] * 3,
        out_specs=VMEM_SPEC,
        compiler_params=kernel_params(),
        name="correct",
    )(*near(low, high, inner))

    state = lax.all_to_all(outgoing, "member", 0, 0).reshape(members, chunk)

    gathered = pltpu.VMEM((len(pieces) * lines, cells_y), F32)
    stacked = pl.pallas_call(
        stack_kernel, out_shape=gathered, in_specs=[VMEM_SPEC] * len(pieces), out_specs=VMEM_SPEC,
        compiler_params=kernel_params(), name="stack",
    )(*near(*pieces))
    parts = [stacked] + [lax.ppermute(stacked, "slab", shift(slabs, by)) for by in range(1, slabs)]
    observed = pl.pallas_call(
        sum_kernel, out_shape=gathered, in_specs=[VMEM_SPEC] * slabs, out_specs=VMEM_SPEC,
        compiler_params=kernel_params(), name="sum",
    )(*near(*parts))
    partner = lax.ppermute(observed, "member", [(i, i ^ 1) for i in range(shards)])

    steps = max(1, chunk // (3 * cells_y))
    width = chunk // steps
    tile = math.gcd(width, 256)
    if width == 3 * cells_y:
        groups = [[f * cells_y + c for f in range(3)] for c in range(0, cells_y, tile)]
    else:
        groups = [[at] for at in range(0, width, tile)]
    firsts = [i * width + g[0] for i in range(steps) for g in groups]
    first = (slab * shards + member) * chunk
    count = len(groups)
    kept = KEPT * count
    near_shape = (kept, nobs, tile)
    far_shape = (steps * batches * count - kept, nobs, tile)
    taper_near, taper_far = pl.pallas_call(
        functools.partial(taper_kernel, slabs, cells_x, cells_y, batches, tile, count, firsts),
        out_shape=(pltpu.VMEM(near_shape, F32), pltpu.HBM(far_shape, F32)),
        in_specs=[SMEM_SPEC, SMEM_SPEC, VMEM_SPEC, VMEM_SPEC],
        out_specs=(VMEM_SPEC,) * 2,
        compiler_params=kernel_params(),
        name="taper",
    )(first.reshape(1), owner, obs_offset, taper_cutoff)

    chain = pl.pallas_call(
        functools.partial(chain_kernel, slabs, cells_x, cells_y, batches, shards),
        out_shape=(
            pltpu.VMEM((batches, nobs, 3 * members), BF16),
            pltpu.VMEM((batches, 2 * members, nobs), BF16),
        ),
        in_specs=[SMEM_SPEC, SMEM_SPEC] + [VMEM_SPEC] * 7,
        out_specs=(VMEM_SPEC,) * 2,
        scratch_shapes=[
            pltpu.VMEM((members, batches * nobs), F32),
            pltpu.VMEM((members, 2 * members), F32),
        ],
        compiler_params=kernel_params(),
        name="chain",
    )
    y_all, w_all = chain(
        member.reshape(1), owner, obs_offset, taper_cutoff, obs_values, obs_variance, perturb, *near(observed, partner))

    return pl.pallas_call(
        functools.partial(update_kernel, batches, tile, groups, width),
        out_shape=jax.ShapeDtypeStruct((members, chunk), F32),
        in_specs=[VMEM_SPEC] * 4 + [ANY_SPEC],
        out_specs=ANY_SPEC,
        scratch_shapes=[
            pltpu.VMEM((members, chunk), F32), pltpu.VMEM(far_shape, F32),
            pltpu.SemaphoreType.DMA((2 * steps,)),
        ],
        compiler_params=kernel_params(),
        name="update",
    )(*near(state, y_all, w_all, taper_near), *far(taper_far))


def solution(mesh):
    in_specs = (P("member", "slab", None, None), P(), P(), P(), P(), P(), P())
    out_specs = P(None, ("slab", "member"))

    return jax.shard_map(on_device, mesh=mesh, in_specs=in_specs, out_specs=out_specs, check_vma=False)
```
